32 devices in a mesh: groups: 2 (over y), tm: 4 (over z), dp: 2 (over x), head: 2 (over core).
Axes of the slice: x: 2, y: 2, z: 4, core: 2. Of those that a mesh axis runs over, the one named last changes fastest.
Arguments:
- frames: bfloat16 [4, 7168, 512], P(('groups', 'dp'), 'tm', 'head'), parts along dimension 0, may hold values from -8 to 8
- lengths: int32 [4], P(('groups', 'dp')), parts along dimension 0, may hold values from 1792 to 7168, as said below
- down_weights: float32 [4, 512], P(None, 'head'), may hold values from 0.1 to 0.4
- w_query: bfloat16 [512, 256], P(None, 'head'), may hold values from -0.79549513 to 0.79549513
- w_key: bfloat16 [512, 256], P(None, 'head'), may hold values from -0.79549513 to 0.79549513
- w_value: bfloat16 [512, 96], P(None, 'head'), may hold values from -0.25 to 0.25
- w_out: bfloat16 [96, 512], P('head'), may hold values from -0.625 to 0.625
- conv_in: bfloat16 [512, 2, 512], P(None, None, 'head'), may hold values from -0.25 to 0.25
- conv_taps: float32 [31, 512], P(None, 'head'), may hold values from -1.8 to 1.8
- conv_out: bfloat16 [512, 512], P('head'), may hold values from -0.25 to 0.25
- bypass: float32 [512], P('head'), may hold values from 0.2 to 0.9
Outputs:
- stack_out: bfloat16 [4, 7168, 512], P(('groups', 'dp'), 'tm', 'head'), parts along dimension 0
The draws below stay inside these ranges and needn't reach their ends.
There are 2 independent parts, one for each index of `groups`. The reference program is written for one: setup_inputs(seed, part) draws one part's arguments, and reference() takes and returns one part's arrays. A program takes and returns all parts, laid end to end along the dimension named above; an argument that names none is the same for every part. Nothing has to cross between parts.
Inputs may be any that keep to these rules, and one draw needn't show every extreme that they name: `lengths`: valid frames of each recording; the later slots are padding. In every part some recording has all 7168 frames.
All inputs are finite; a program needn't handle non-finite values.
Results may differ from the reference program's by a relative error of at most 0.009.
Values may be sent and summed in bfloat16 or wider, within the bound.
No kernel may reach another device: no remote copies, remote signals or barrier semaphores. Data moves between devices by JAX's collectives and lax.ppermute only.
A program may use at most 64 MiB of HBM per device.

```python
import math
import jax
import jax.numpy as jnp
from jax import lax

D = 512
HEADS = 8
QDIM = 32
VDIM = 12
KERNEL = 31
B = 2
T_SIZE = 7168
N_TM = 4


def draw_frames(key, part):
    return jnp.clip(jax.random.normal(jax.random.fold_in(key, 6), (B, T_SIZE, D), jnp.float32), -6.0, 6.0).astype(jnp.bfloat16)


def draw_lengths(key, part):
    drawn = jax.random.randint(jax.random.fold_in(key, 21), (B,), T_SIZE // 4, T_SIZE + 1)
    longest = jax.random.randint(jax.random.fold_in(key, 22), (), 0, B)
    return jnp.where(jnp.arange(B) == longest, T_SIZE, drawn).astype(jnp.int32)


def query_key_parts(key):
    own_query = jax.random.normal(jax.random.fold_in(key, 32), (D, HEADS * QDIM), jnp.float32)
    own_key = jax.random.normal(jax.random.fold_in(key, 33), (D, HEADS * QDIM), jnp.float32)
    return (own_query, own_key)


def draw_w_query(key, part):
    own_query, own_key = query_key_parts(key)
    blended = own_query
    return (jnp.clip(blended, -6.0, 6.0) * (3.0 / math.sqrt(D))).astype(jnp.bfloat16)


def draw_w_key(key, part):
    own_query, own_key = query_key_parts(key)
    blended = own_key
    return (jnp.clip(blended, -6.0, 6.0) * (3.0 / math.sqrt(D))).astype(jnp.bfloat16)


def shard_levels(rng, extent, pieces, smallest, top_value):
    def one(axis_at, parts):
        draws = jax.random.uniform(jax.random.fold_in(jax.random.fold_in(rng, 6), axis_at), (parts,), jnp.float32, smallest / len(pieces), top_value / len(pieces))
        return jnp.repeat(jnp.exp(draws), extent[axis_at] // parts).reshape((-1,) + (1,) * (len(extent) - axis_at - 1))

    loudness = one(*pieces[0])
    for cut in pieces[1:]:
        loudness = loudness * one(*cut)
    return loudness


def bell_draw(rng, extent, spread, limit, pieces=(), held_as=jnp.bfloat16):
    values = spread * jax.random.normal(rng, extent, jnp.float32)
    if pieces:
        values = values * shard_levels(rng, extent, pieces, -0.22, 0.18)
    return jnp.clip(values, -limit, limit).astype(held_as)


def setup_inputs(seed: int = 0, part: int = 0) -> dict:
    key_list = jax.random.split(jax.random.key(seed), 12)
    own_keys = jax.random.split(jax.random.fold_in(key_list[11], part), 12)
    return {
        "frames": draw_frames(jax.random.fold_in(jax.random.fold_in(key_list[11], part), 71), part),
        "lengths": draw_lengths(jax.random.fold_in(jax.random.fold_in(key_list[11], part), 71), part),
        "down_weights": jnp.clip(0.1 + 0.3 * jax.random.uniform(key_list[2], (4, D), jnp.float32) ** shard_levels(key_list[2], (4, D), ((1, 2),), -0.2, 0.2), 0.1, 0.4),
        "w_query": draw_w_query(jax.random.fold_in(key_list[11], 71), part),
        "w_key": draw_w_key(jax.random.fold_in(key_list[11], 71), part),
        "w_value": bell_draw(key_list[5], (D, HEADS * VDIM), D ** -0.5, 0.25, ((1, 2),)),
        "w_out": bell_draw(key_list[6], (HEADS * VDIM, D), (HEADS * VDIM) ** -0.5, 0.625, ((0, 2),)),
        "conv_in": bell_draw(key_list[7], (D, 2, D), D ** -0.5, 0.25, ((2, 2),)),
        "conv_taps": bell_draw(key_list[8], (KERNEL, D), 0.3, 1.8, ((1, 2),), jnp.float32),
        "conv_out": bell_draw(key_list[9], (D, D), D ** -0.5, 0.25, ((0, 2),)),
        "bypass": jnp.clip(0.2 + 0.7 * jax.random.uniform(key_list[10], (D,), jnp.float32) ** shard_levels(key_list[10], (D,), ((0, 2),), -0.2, 0.2), 0.2, 0.9),
    }


def rounded(value):
    return lax.optimization_barrier(value.astype(jnp.bfloat16)).astype(jnp.float32)


def attend_one(queries, keys, values, live_count):
    row_count = keys.shape[0]
    key_valid = jnp.arange(row_count) < live_count
    blocks = queries.reshape(N_TM, row_count // N_TM, HEADS, QDIM)

    def one_block(query_block):
        scores = jnp.einsum('qhd,khd->hqk', query_block, keys) * (QDIM ** -0.5)
        scores = jnp.where(key_valid[None, None, :], scores, -jnp.inf)
        row_top = jnp.max(scores, axis=-1, keepdims=True)
        expo = jnp.exp(scores - row_top)
        denominator = jnp.sum(expo, axis=-1)
        numerator = jnp.einsum('hqk,khv->qhv', rounded(expo), values)
        return numerator / jnp.transpose(denominator)[:, :, None]

    return lax.map(one_block, blocks).reshape(row_count, HEADS, VDIM)


def reference(frames, lengths, down_weights, w_query, w_key, w_value, w_out, conv_in, conv_taps, conv_out, bypass):
    records, frame_total, width = frames.shape
    row_count = frame_total // 4
    frame_live = jnp.arange(frame_total)[None, :] < lengths[:, None]
    masked = jnp.where(frame_live[:, :, None], frames.astype(jnp.float32), jnp.float32(0.0))
    reduced = jnp.sum(masked.reshape(records, row_count, 4, width) * down_weights[None, None], axis=2).astype(jnp.bfloat16)
    flattened = reduced.reshape(records * row_count, width)
    queries = rounded(jnp.dot(flattened, w_query, preferred_element_type=jnp.float32)).reshape(records, row_count, HEADS, QDIM)
    keys = rounded(jnp.dot(flattened, w_key, preferred_element_type=jnp.float32)).reshape(records, row_count, HEADS, QDIM)
    values = rounded(jnp.dot(flattened, w_value, preferred_element_type=jnp.float32)).reshape(records, row_count, HEADS, VDIM)
    live_rows = ((lengths + 3) // 4).astype(jnp.int32)
    attended = lax.map(lambda packed: attend_one(packed[0], packed[1], packed[2], packed[3]), (queries, keys, values, live_rows))
    attended = attended.astype(jnp.bfloat16).reshape(records * row_count, HEADS * VDIM)
    after_attn = (flattened.astype(jnp.float32) + jnp.dot(attended, w_out, preferred_element_type=jnp.float32)).astype(jnp.bfloat16)
    gates = jnp.dot(after_attn, conv_in.reshape(width, 2 * width), preferred_element_type=jnp.float32).reshape(records, row_count, 2, width)
    row_live = jnp.arange(row_count)[None, :] < live_rows[:, None]
    gated = gates[:, :, 0] * jax.nn.sigmoid(gates[:, :, 1])
    gated = rounded(jnp.where(row_live[:, :, None], gated, jnp.float32(0.0)))
    reach = KERNEL // 2
    padded = jnp.pad(gated, ((0, 0), (reach, reach), (0, 0)))
    depthwise = jnp.zeros((records, row_count, width), jnp.float32)
    for tap_index in range(KERNEL):
        depthwise = depthwise + conv_taps[tap_index][None, None, :] * padded[:, tap_index:tap_index + row_count]
    hidden = jax.nn.silu(depthwise).astype(jnp.bfloat16).reshape(records * row_count, width)
    stacked = after_attn.astype(jnp.float32) + jnp.dot(hidden, conv_out, preferred_element_type=jnp.float32)
    upsampled = jnp.repeat(stacked.reshape(records, row_count, width), 4, axis=1)
    backdrop = frames.astype(jnp.float32)
    result = backdrop + bypass[None, None, :] * (upsampled - backdrop)
    return jnp.where(frame_live[:, :, None], result, jnp.float32(0.0)).astype(jnp.bfloat16)
```

```python
import functools
import math

import jax
import jax.numpy as jnp
from jax import lax
from jax.experimental import pallas as pl
from jax.experimental.pallas import tpu as pltpu
from jax.sharding import PartitionSpec as P

QDIM = 32
VDIM = 12
NEG = -1e30
F32 = jnp.float32
BF16 = jnp.bfloat16
VM = pl.BlockSpec(memory_space=pltpu.VMEM)
SM = pl.BlockSpec(memory_space=pltpu.SMEM)
HB = pl.BlockSpec(memory_space=pl.ANY)
NT = (((1,), (1,)), ((), ()))
TN = (((0,), (0,)), ((), ()))


def in_vmem(array):
    return pltpu.with_memory_space_constraint(array, pltpu.VMEM)


def call(kernel, outs, operands, specs, name, scratch=(), flops=0, moved=0, exps=0):
    out_specs = [VM] * len(outs)
    operands = [in_vmem(a) if s is VM else a for a, s in zip(operands, specs)]
    return pl.pallas_call(
        kernel,
        out_shape=outs,
        in_specs=specs,
        out_specs=out_specs,
        scratch_shapes=list(scratch),
        name=name,
        cost_estimate=pl.CostEstimate(flops=flops, bytes_accessed=moved, transcendentals=exps),
    )(*operands)


def dot(a, b, dims=None):
    if dims is None:
        return jnp.dot(a, b, preferred_element_type=F32)
    return lax.dot_general(a, b, dims, preferred_element_type=F32)


def halves(channels):
    here = lax.axis_index("head")
    mine = pl.ds(pl.multiple_of(here * channels, channels), channels)
    theirs = pl.ds(pl.multiple_of((1 - here) * channels, channels), channels)
    return mine, theirs


def down_kernel(parts, len_ref, frames_ref, weights_ref, out_ref, info_ref, raw, wide, sems):
    frame_count, channels = raw.shape
    tiles = channels // 128
    step = frame_count // parts
    rows = step // 4
    copies = [
        pltpu.make_async_copy(
            frames_ref.at[pl.ds(i * step, step)], raw.at[pl.ds(i * step, step)], sems.at[i]
        )
        for i in range(parts)
    ]
    for copy in copies:
        copy.start()
    length = len_ref[0]
    live_rows = lax.shift_right_logical(length + 3, 2)
    which = lax.broadcasted_iota(jnp.int32, info_ref.shape, 0)
    info_ref[...] = jnp.where(which == 0, live_rows, length)
    first = lax.axis_index("tm") * frame_count
    for i in range(parts):
        copies[i].wait()
        base = first + i * step
        row = base + 4 * lax.broadcasted_iota(jnp.int32, (rows, 128), 0)
        for tile in range(tiles):
            lanes = slice(tile * 128, tile * 128 + 128)
            wide[tile, i * step : (i + 1) * step] = raw[i * step : (i + 1) * step, lanes].astype(F32)
            total = None
            for j in range(4):
                part = wide[tile, pl.ds(i * step + j, rows, stride=4), :]
                part = jnp.where(row + j < length, part, 0.0) * weights_ref[j : j + 1, lanes]
                total = part if total is None else total + part
            out_ref[i * rows : (i + 1) * rows, lanes] = total.astype(BF16)


def pack_rows(quarter, width):
    return quarter + width * ((quarter + 127) // 128)


def kv_kernel(halo, mine_ref, theirs_ref, wk_ref, wvt_ref, pack_ref, head_ref, tail_ref):
    quarter, channels = mine_ref.shape
    width = wvt_ref.shape[0]
    mine, theirs = halves(channels)
    a, b = mine_ref[...], theirs_ref[...]
    keys = dot(a, wk_ref[mine, :]) + dot(b, wk_ref[theirs, :])
    pack_ref[:quarter, :] = keys.astype(BF16)
    values_t = dot(wvt_ref[:, mine], a, NT) + dot(wvt_ref[:, theirs], b, NT)
    values_t = values_t.astype(BF16)
    at = quarter
    for lane in range(0, quarter, 128):
        size = min(128, quarter - lane)
        if size < 128:
            pack_ref[at : at + width, :] = jnp.zeros((width, 128), BF16)
        pack_ref[at : at + width, :size] = values_t[:, lane : lane + size]
        at += width
    head_ref[:, :channels] = mine_ref[:halo, :]
    head_ref[:, channels:] = theirs_ref[:halo, :]
    tail_ref[:, :channels] = mine_ref[quarter - halo :, :]
    tail_ref[:, channels:] = theirs_ref[quarter - halo :, :]


def head_query(q_t, head):
    at = lax.broadcasted_iota(jnp.int32, q_t.shape, 0) // QDIM
    return jnp.where(at == head, q_t, 0.0).astype(BF16)


def head_values(pack, quarter, heads, head):
    width = heads * VDIM
    pieces = []
    at = quarter
    for lane in range(0, quarter, 128):
        size = min(128, quarter - lane)
        pieces.append(pack[at : at + width, :size].astype(F32))
        at += width
    values_t = jnp.concatenate(pieces, axis=1)
    row = lax.broadcasted_iota(jnp.int32, (width, quarter), 0)
    low, high = head * VDIM, (head + 1) * VDIM
    kept = jnp.where((row >= low) & (row < high), values_t, 0.0).astype(BF16)
    extra = lax.broadcasted_iota(jnp.int32, (16, quarter), 0)
    ones = jnp.where(extra == head, 1.0, 0.0).astype(BF16)
    return jnp.concatenate([kept, ones], axis=0)


def spread(rows, shape, heads):
    at = lax.broadcasted_iota(jnp.int32, shape, 0)
    out = jnp.broadcast_to(rows[0], shape)
    for head in range(1, heads):
        ours = (at >= head * VDIM) & (at < (head + 1) * VDIM) | (at == heads * VDIM + head)
        out = jnp.where(ours, jnp.broadcast_to(rows[head], shape), out)
    return out


def absorb(q_t, packs, sources, live_rows, quarter, heads, before, score_ref):
    queries = q_t.shape[1]
    row = lax.broadcasted_iota(jnp.int32, (quarter, queries), 0)
    tops, factors, total = [], [], None
    for head in range(heads):
        query = head_query(q_t, head)
        top = None if before is None else before[0][head]
        for i, (pack, source) in enumerate(zip(packs, sources)):
            scores = dot(pack[:quarter, :], query)
            scores = jnp.where(row < live_rows - source * quarter, scores, NEG)
            score_ref[i * quarter : (i + 1) * quarter, :] = scores
            best = jnp.max(scores, axis=0, keepdims=True)
            top = best if top is None else jnp.maximum(top, best)
        for i, pack in enumerate(packs):
            expo = jnp.exp2(score_ref[i * quarter : (i + 1) * quarter, :] - top).astype(BF16)
            part = dot(head_values(pack, quarter, heads, head), expo)
            total = part if total is None else total + part
        if before is not None:
            factors.append(jnp.exp2(before[0][head] - top))
        tops.append(top)
    if before is not None:
        total = total + before[1] * spread(factors, total.shape, heads)
    return tops, total


def finish(total, heads):
    width = heads * VDIM
    down = [total[width + head : width + head + 1, :] for head in range(heads)]
    return total[:width, :] / spread(down, (width, total.shape[1]), heads)


def open_kernel(heads, shifts, last, info_ref, mine_ref, theirs_ref, left_ref, right_ref, wq_ref, *rest):
    packs = rest[: len(shifts)]
    rows_ref, qt_ref, top_ref, sum_ref, score_ref = rest[len(shifts) :]
    quarter, channels = mine_ref.shape
    halo = left_ref.shape[0]
    queries = rows_ref.shape[0]
    rows_ref[:halo, :] = left_ref[...]
    rows_ref[halo : halo + quarter, :channels] = mine_ref[...]
    rows_ref[halo : halo + quarter, channels:] = theirs_ref[...]
    rows_ref[halo + quarter : 2 * halo + quarter, :] = right_ref[...]
    rows_ref[2 * halo + quarter :, :] = jnp.zeros((queries - 2 * halo - quarter, 2 * channels), BF16)
    mine, theirs = halves(channels)
    query = dot(rows_ref[:, :channels], wq_ref[mine, :]) + dot(rows_ref[:, channels:], wq_ref[theirs, :])
    q_t = jnp.transpose(query * (math.log2(math.e) / math.sqrt(QDIM)))
    qt_ref[...] = q_t
    here = lax.axis_index("tm")
    count = lax.axis_size("tm")
    sources = [lax.rem(here + shift + count, count) for shift in shifts]
    tops, total = absorb(
        q_t, packs, sources, info_ref[0:1, 0:1], quarter, heads, None, score_ref
    )
    for head in range(heads):
        top_ref[head : head + 1, :] = tops[head]
    sum_ref[...] = total


def more_kernel(heads, shifts, last, info_ref, qt_ref, top_in_ref, sum_in_ref, *rest):
    packs = rest[: len(shifts)]
    outs = rest[len(shifts) : -1]
    score_ref = rest[-1]
    quarter = score_ref.shape[0] // len(shifts)
    here = lax.axis_index("tm")
    count = lax.axis_size("tm")
    sources = [lax.rem(here + shift + count, count) for shift in shifts]
    before = ([top_in_ref[head : head + 1, :] for head in range(heads)], sum_in_ref[...])
    tops, total = absorb(
        qt_ref[...], packs, sources, info_ref[0:1, 0:1], quarter, heads, before, score_ref
    )
    if last:
        outs[0][...] = finish(total, heads).astype(BF16)
    else:
        for head in range(heads):
            outs[0][head : head + 1, :] = tops[head]
        outs[1][...] = total


def conv_kernel(
    halo, info_ref, rows_ref, mine_att_ref, their_att_ref, mine_out_ref, their_out_ref, conv_in_ref,
    taps_ref, after_ref, hidden_ref, gated,
):
    quarter, channels = hidden_ref.shape
    taps = taps_ref.shape[0]
    count = quarter + 2 * halo
    mine, theirs = halves(channels)
    attended = jnp.concatenate([mine_att_ref[...], their_att_ref[...]], axis=0)
    sides = []
    for side, lanes in ((mine, slice(0, channels)), (theirs, slice(channels, 2 * channels))):
        w_out = jnp.concatenate([mine_out_ref[:, side], their_out_ref[:, side]], axis=0)
        delta = dot(attended, w_out, TN)
        sides.append((rows_ref[:, lanes].astype(F32) + delta).astype(BF16)[:count])
    after_ref[...] = sides[0][halo : halo + quarter]
    gates = dot(sides[0], conv_in_ref[mine, :]) + dot(sides[1], conv_in_ref[theirs, :])
    value, gate = gates[:, :channels], gates[:, channels:]
    row = lax.broadcasted_iota(jnp.int32, (count, channels), 0)
    row = row + (lax.axis_index("tm") * quarter - halo)
    live = (row >= 0) & (row < info_ref[0:1, 0:1])
    mixed = jnp.where(live, value * jax.nn.sigmoid(gate), 0.0).astype(BF16).astype(F32)
    for tile in range(channels // 128):
        gated[tile] = mixed[:, tile * 128 : (tile + 1) * 128]
    block = 64
    start = halo - taps // 2
    for tile in range(channels // 128):
        lanes = slice(tile * 128, tile * 128 + 128)
        for base in range(0, quarter, block):
            total = None
            for k in range(taps):
                part = gated[tile, base + k + start : base + k + start + block, :] * taps_ref[k : k + 1, lanes]
                total = part if total is None else total + part
            hidden_ref[base : base + block, lanes] = (total * jax.nn.sigmoid(total)).astype(BF16)


def half_kernel(after_ref, hidden_ref, out_w_ref, base_ref):
    channels = hidden_ref.shape[1]
    mine, _ = halves(channels)
    base_ref[...] = after_ref[...].astype(F32) + dot(hidden_ref[...], out_w_ref[:, mine])


def last_kernel(info_ref, base_ref, hidden_ref, out_w_ref, frames_ref, bypass_ref, out_ref, tall):
    quarter, channels = base_ref.shape
    frame_count = frames_ref.shape[0]
    mine, _ = halves(channels)
    stacked = base_ref[...] + dot(hidden_ref[...], out_w_ref[:, mine])
    length = info_ref[1:2, 0:1]
    at = lax.broadcasted_iota(jnp.int32, (frame_count, 128), 0) + lax.axis_index("tm") * frame_count
    live = at < length
    for tile in range(channels // 128):
        lanes = slice(tile * 128, tile * 128 + 128)
        for j in range(4):
            tall[tile, pl.ds(j, quarter, stride=4), :] = stacked[:, lanes]
        backdrop = frames_ref[:, lanes].astype(F32)
        result = backdrop + bypass_ref[:, lanes] * (tall[tile] - backdrop)
        out_ref[:, lanes] = jnp.where(live, result, 0.0).astype(BF16)


def shards(
    frames,
    lengths,
    down_weights,
    w_query,
    w_key,
    w_value,
    w_out,
    conv_in,
    conv_taps,
    conv_out,
    bypass,
):
    records, frame_count, channels = frames.shape
    quarter = frame_count // 4
    heads = w_query.shape[1] // QDIM
    keys_wide = w_query.shape[1]
    count = lax.axis_size("tm")
    halo = -(-(conv_taps.shape[0] // 2) // 16) * 16
    queries = -(-(quarter + 2 * halo) // 128) * 128
    frames = frames.reshape(frame_count, channels)
    swap = [(0, 1), (1, 0)]

    def ring(array, by):
        return lax.ppermute(array, "tm", [(i, (i + by) % count) for i in range(count)])

    def vmem(shape, dtype):
        return pltpu.VMEM(shape, dtype)

    reduced, info = call(
        functools.partial(down_kernel, 4),
        [vmem((quarter, channels), BF16), vmem((8, 128), jnp.int32)],
        [lengths, frames, down_weights],
        [SM, HB, VM],
        "down",
        [
            pltpu.VMEM((frame_count, channels), BF16),
            pltpu.VMEM((channels // 128, frame_count, 128), F32),
            pltpu.SemaphoreType.DMA((4,)),
        ],
        flops=8 * frame_count * channels,
        moved=3 * frame_count * channels,
    )
    theirs = lax.ppermute(reduced, "head", swap)
    pack, head_rows, tail_rows = call(
        functools.partial(kv_kernel, halo),
        [
            vmem((pack_rows(quarter, heads * VDIM), keys_wide), BF16),
            vmem((halo, 2 * channels), BF16),
            vmem((halo, 2 * channels), BF16),
        ],
        [reduced, theirs, w_key, w_value.T],
        [VM] * 4,
        "keys_values",
        flops=4 * quarter * channels * (keys_wide + heads * VDIM),
        moved=8 * quarter * channels,
    )
    right = [pack]
    left = [pack]
    steps_right, steps_left = count // 2, (count - 1) // 2
    if steps_right:
        right.append(ring(pack, 1))
    if steps_left:
        left.append(ring(pack, -1))
    left_rows = ring(tail_rows, 1)
    right_rows = ring(head_rows, -1)
    for step in range(2, steps_right + 1):
        right.append(ring(right[-1], 1))
    for step in range(2, steps_left + 1):
        left.append(ring(left[-1], -1))
    their_w_out = lax.ppermute(w_out, "head", swap)
    their_conv_out = lax.ppermute(conv_out, "head", swap)

    stages = [[(0, pack)]]
    for step in range(1, steps_right + 1):
        stage = [(-step, right[step])]
        if step <= steps_left:
            stage.append((step, left[step]))
        stages.append(stage)
    if len(stages) > 1:
        stages = [stages[0] + stages[1]] + stages[2:]
    score_flops = 2 * quarter * queries * heads * (128 + 64)

    first = stages[0]
    rows, q_t, top, total = call(
        functools.partial(open_kernel, heads, [shift for shift, _ in first], False),
        [
            vmem((queries, 2 * channels), BF16),
            vmem((keys_wide, queries), F32),
            vmem((8, queries), F32),
            vmem((heads * VDIM + 16, queries), F32),
        ],
        [info, reduced, theirs, left_rows, right_rows, w_query] + [array for _, array in first],
        [VM] * (6 + len(first)),
        "attend_first",
        [pltpu.VMEM((len(first) * quarter, queries), F32)],
        flops=score_flops * len(first),
        moved=quarter * queries * 4,
        exps=quarter * queries * heads * len(first),
    )
    for index, stage in enumerate(stages[1:]):
        last = index == len(stages) - 2
        outs = [vmem((8, queries), F32), vmem((heads * VDIM + 16, queries), F32)]
        if last:
            outs = [vmem((heads * VDIM, queries), BF16)]
        state = call(
            functools.partial(more_kernel, heads, [shift for shift, _ in stage], last),
            outs,
            [info, q_t, top, total] + [array for _, array in stage],
            [VM] * (4 + len(stage)),
            "attend_more",
            [pltpu.VMEM((len(stage) * quarter, queries), F32)],
            flops=score_flops * len(stage),
            moved=quarter * queries * 4,
            exps=quarter * queries * heads * len(stage),
        )
        if last:
            attended = state[0]
        else:
            top, total = state
    their_attended = lax.ppermute(attended, "head", swap)
    after, hidden = call(
        functools.partial(conv_kernel, halo),
        [vmem((quarter, channels), BF16), vmem((quarter, channels), BF16)],
        [
            info, rows, attended, their_attended, w_out, their_w_out,
            conv_in.reshape(2 * channels, 2 * channels), conv_taps,
        ],
        [VM] * 8,
        "gate_conv",
        [pltpu.VMEM((channels // 128, quarter + 2 * halo, 128), F32)],
        flops=2 * queries * 2 * channels * (96 + 2 * channels),
        moved=quarter * channels * 8,
    )
    their_hidden = lax.ppermute(hidden, "head", swap)
    (base,) = call(
        half_kernel,
        [vmem((quarter, channels), F32)],
        [after, hidden, conv_out],
        [VM] * 3,
        "half_out",
        flops=2 * quarter * channels * channels,
        moved=quarter * channels * 4,
    )
    (out,) = call(
        last_kernel,
        [jax.ShapeDtypeStruct((frame_count, channels), BF16)],
        [info, base, their_hidden, their_conv_out, frames, bypass.reshape(1, channels)],
        [VM] * 6,
        "bypass",
        [pltpu.VMEM((channels // 128, frame_count, 128), F32)],
        flops=2 * quarter * channels * channels,
        moved=frame_count * channels * 4,
    )
    return out.reshape(records, frame_count, channels)


def solution(mesh):
    in_specs = (
        P(("groups", "dp"), "tm", "head"),
        P(("groups", "dp")),
        P(None, "head"),
        P(None, "head"),
        P(None, "head"),
        P(None, "head"),
        P("head", None),
        P(None, None, "head"),
        P(None, "head"),
        P("head", None),
        P("head"),
    )
    out_specs = P(("groups", "dp"), "tm", "head")
    return jax.shard_map(shards, mesh=mesh, in_specs=in_specs, out_specs=out_specs, check_vma=False)
```

```python
import functools
import math

import jax
import jax.numpy as jnp
from jax import lax
from jax.experimental import pallas as pl
from jax.experimental.pallas import tpu as pltpu
from jax.sharding import PartitionSpec as P

QDIM = 32
VDIM = 12
NEG = -1e30
F32 = jnp.float32
BF16 = jnp.bfloat16
VM = pl.BlockSpec(memory_space=pltpu.VMEM)
SM = pl.BlockSpec(memory_space=pltpu.SMEM)
HB = pl.BlockSpec(memory_space=pl.ANY)
NT = (((1,), (1,)), ((), ()))
TN = (((0,), (0,)), ((), ()))


def in_vmem(array):
    return pltpu.with_memory_space_constraint(array, pltpu.VMEM)


def call(kernel, outs, operands, specs, name, scratch=(), out_specs=None, flops=0, moved=0, exps=0):
    out_specs = out_specs or [VM] * len(outs)
    operands = [in_vmem(a) if s is VM else a for a, s in zip(operands, specs)]
    return pl.pallas_call(
        kernel,
        out_shape=outs,
        in_specs=specs,
        out_specs=out_specs,
        scratch_shapes=list(scratch),
        name=name,
        cost_estimate=pl.CostEstimate(flops=flops, bytes_accessed=moved, transcendentals=exps),
    )(*operands)


def dot(a, b, dims=None):
    if dims is None:
        return jnp.dot(a, b, preferred_element_type=F32)
    return lax.dot_general(a, b, dims, preferred_element_type=F32)


def halves(channels):
    here = lax.axis_index("head")
    mine = pl.ds(pl.multiple_of(here * channels, channels), channels)
    theirs = pl.ds(pl.multiple_of((1 - here) * channels, channels), channels)
    return mine, theirs


def down_kernel(parts, len_ref, frames_ref, weights_hbm, out_ref, info_ref, raw, wide, weights_ref, sems):
    frame_count, channels = raw.shape
    tiles = channels // 128
    step = frame_count // parts
    rows = step // 4
    copies = [
        pltpu.make_async_copy(
            frames_ref.at[pl.ds(i * step, step)], raw.at[pl.ds(i * step, step)], sems.at[i]
        )
        for i in range(parts)
    ]
    weights_copy = pltpu.make_async_copy(weights_hbm, weights_ref, sems.at[parts])
    weights_copy.start()
    for copy in copies:
        copy.start()
    length = len_ref[0]
    live_rows = lax.shift_right_logical(length + 3, 2)
    which = lax.broadcasted_iota(jnp.int32, info_ref.shape, 0)
    info_ref[...] = jnp.where(which == 0, live_rows, length)
    first = lax.axis_index("tm") * frame_count
    weights_copy.wait()
    for i in range(parts):
        copies[i].wait()
        base = first + i * step
        row = base + 4 * lax.broadcasted_iota(jnp.int32, (rows, 128), 0)
        for tile in range(tiles):
            lanes = slice(tile * 128, tile * 128 + 128)
            wide[tile, i * step : (i + 1) * step] = raw[i * step : (i + 1) * step, lanes].astype(F32)
            total = None
            for j in range(4):
                part = wide[tile, pl.ds(i * step + j, rows, stride=4), :]
                part = jnp.where(row + j < length, part, 0.0) * weights_ref[j : j + 1, lanes]
                total = part if total is None else total + part
            out_ref[i * rows : (i + 1) * rows, lanes] = total.astype(BF16)


def kv_rows(quarter, width):
    return quarter + width * ((quarter + 127) // 128)


def put_edge(pack_ref, at, halo, rows):
    for i in range(rows.shape[1] // 128):
        pack_ref[at + i * halo : at + (i + 1) * halo, :] = rows[:, i * 128 : (i + 1) * 128]
    return at + halo * (rows.shape[1] // 128)


def get_edge(pack_ref, at, halo, width):
    pieces = [pack_ref[at + i * halo : at + (i + 1) * halo, :] for i in range(width // 128)]
    return jnp.concatenate(pieces, axis=1)


def kv_kernel(halo, mine_ref, theirs_ref, wk_ref, wvt_ref, right_ref, left_ref):
    quarter, channels = mine_ref.shape
    width = wvt_ref.shape[0]
    mine, theirs = halves(channels)
    a, b = mine_ref[...], theirs_ref[...]
    keys = dot(a, wk_ref[mine, :]) + dot(b, wk_ref[theirs, :])
    keys = keys.astype(BF16)
    values_t = dot(wvt_ref[:, mine], a, NT) + dot(wvt_ref[:, theirs], b, NT)
    values_t = values_t.astype(BF16)
    for pack_ref, edge in ((right_ref, slice(quarter - halo, quarter)), (left_ref, slice(0, halo))):
        pack_ref[:quarter, :] = keys
        at = quarter
        for lane in range(0, quarter, 128):
            size = min(128, quarter - lane)
            if size < 128:
                pack_ref[at : at + width, :] = jnp.zeros((width, 128), BF16)
            pack_ref[at : at + width, :size] = values_t[:, lane : lane + size]
            at += width
        at = put_edge(pack_ref, at, halo, mine_ref[edge, :])
        put_edge(pack_ref, at, halo, theirs_ref[edge, :])


def head_query(q_t, head):
    at = lax.broadcasted_iota(jnp.int32, q_t.shape, 0) // QDIM
    return jnp.where(at == head, q_t, 0.0).astype(BF16)


def head_values(pack, quarter, heads, head):
    width = heads * VDIM
    pieces = []
    at = quarter
    for lane in range(0, quarter, 128):
        size = min(128, quarter - lane)
        pieces.append(pack[at : at + width, :size].astype(F32))
        at += width
    values_t = jnp.concatenate(pieces, axis=1)
    row = lax.broadcasted_iota(jnp.int32, (width, quarter), 0)
    low, high = head * VDIM, (head + 1) * VDIM
    kept = jnp.where((row >= low) & (row < high), values_t, 0.0).astype(BF16)
    extra = lax.broadcasted_iota(jnp.int32, (16, quarter), 0)
    ones = jnp.where(extra == head, 1.0, 0.0).astype(BF16)
    return jnp.concatenate([kept, ones], axis=0)


def spread(rows, shape, heads):
    at = lax.broadcasted_iota(jnp.int32, shape, 0)
    out = jnp.broadcast_to(rows[0], shape)
    for head in range(1, heads):
        ours = (at >= head * VDIM) & (at < (head + 1) * VDIM) | (at == heads * VDIM + head)
        out = jnp.where(ours, jnp.broadcast_to(rows[head], shape), out)
    return out


def absorb(q_t, packs, sources, live_rows, quarter, heads, before, score_ref):
    queries = q_t.shape[1]
    row = lax.broadcasted_iota(jnp.int32, (quarter, queries), 0)
    tops, factors, total = [], [], None
    for head in range(heads):
        query = head_query(q_t, head)
        top = None if before is None else before[0][head]
        for i, (pack, source) in enumerate(zip(packs, sources)):
            scores = dot(pack[:quarter, :], query)
            scores = jnp.where(row < live_rows - source * quarter, scores, NEG)
            score_ref[i * quarter : (i + 1) * quarter, :] = scores
            best = jnp.max(scores, axis=0, keepdims=True)
            top = best if top is None else jnp.maximum(top, best)
        for i, pack in enumerate(packs):
            expo = jnp.exp2(score_ref[i * quarter : (i + 1) * quarter, :] - top).astype(BF16)
            part = dot(head_values(pack, quarter, heads, head), expo)
            total = part if total is None else total + part
        if before is not None:
            factors.append(jnp.exp2(before[0][head] - top))
        tops.append(top)
    if before is not None:
        total = total + before[1] * spread(factors, total.shape, heads)
    return tops, total


def finish(total, heads):
    width = heads * VDIM
    down = [total[width + head : width + head + 1, :] for head in range(heads)]
    return total[:width, :] / spread(down, (width, total.shape[1]), heads)


def open_kernel(heads, halo, shifts, info_ref, mine_ref, theirs_ref, wq_ref, *rest):
    packs = rest[: len(shifts)]
    rows_ref, qt_ref, top_ref, sum_ref, score_ref = rest[len(shifts) :]
    quarter, channels = mine_ref.shape
    edge = kv_rows(quarter, heads * VDIM)
    queries = rows_ref.shape[0]
    rows_ref[:halo, :] = get_edge(packs[1], edge, halo, 2 * channels)
    rows_ref[halo : halo + quarter, :channels] = mine_ref[...]
    rows_ref[halo : halo + quarter, channels:] = theirs_ref[...]
    rows_ref[halo + quarter : 2 * halo + quarter, :] = get_edge(packs[2], edge, halo, 2 * channels)
    rows_ref[2 * halo + quarter :, :] = jnp.zeros((queries - 2 * halo - quarter, 2 * channels), BF16)
    mine, theirs = halves(channels)
    query = dot(rows_ref[:, :channels], wq_ref[mine, :]) + dot(rows_ref[:, channels:], wq_ref[theirs, :])
    q_t = jnp.transpose(query * (math.log2(math.e) / math.sqrt(QDIM)))
    qt_ref[...] = q_t
    here = lax.axis_index("tm")
    count = lax.axis_size("tm")
    sources = [lax.rem(here + shift + count, count) for shift in shifts]
    tops, total = absorb(
        q_t, packs, sources, info_ref[0:1, 0:1], quarter, heads, None, score_ref
    )
    for head in range(heads):
        top_ref[head : head + 1, :] = tops[head]
    sum_ref[...] = total


def more_kernel(heads, shifts, last, info_ref, qt_ref, top_in_ref, sum_in_ref, *rest):
    packs = rest[: len(shifts)]
    outs = rest[len(shifts) : -1]
    score_ref = rest[-1]
    quarter = score_ref.shape[0] // len(shifts)
    here = lax.axis_index("tm")
    count = lax.axis_size("tm")
    sources = [lax.rem(here + shift + count, count) for shift in shifts]
    before = ([top_in_ref[head : head + 1, :] for head in range(heads)], sum_in_ref[...])
    tops, total = absorb(
        qt_ref[...], packs, sources, info_ref[0:1, 0:1], quarter, heads, before, score_ref
    )
    if last:
        outs[0][...] = finish(total, heads).astype(BF16)
    else:
        for head in range(heads):
            outs[0][head : head + 1, :] = tops[head]
        outs[1][...] = total


def conv_kernel(
    halo, info_ref, rows_ref, mine_att_ref, their_att_ref, mine_out_ref, their_out_ref, conv_in_ref,
    taps_ref, after_ref, hidden_ref, gated,
):
    quarter, channels = hidden_ref.shape
    taps = taps_ref.shape[0]
    count = quarter + 2 * halo
    mine, theirs = halves(channels)
    attended = jnp.concatenate([mine_att_ref[...], their_att_ref[...]], axis=0)
    sides = []
    for side, lanes in ((mine, slice(0, channels)), (theirs, slice(channels, 2 * channels))):
        w_out = jnp.concatenate([mine_out_ref[:, side], their_out_ref[:, side]], axis=0)
        delta = dot(attended, w_out, TN)
        sides.append((rows_ref[:, lanes].astype(F32) + delta).astype(BF16)[:count])
    after_ref[...] = sides[0][halo : halo + quarter]
    gates = dot(sides[0], conv_in_ref[mine, :]) + dot(sides[1], conv_in_ref[theirs, :])
    value, gate = gates[:, :channels], gates[:, channels:]
    row = lax.broadcasted_iota(jnp.int32, (count, channels), 0)
    row = row + (lax.axis_index("tm") * quarter - halo)
    live = (row >= 0) & (row < info_ref[0:1, 0:1])
    mixed = jnp.where(live, value * jax.nn.sigmoid(gate), 0.0).astype(BF16).astype(F32)
    for tile in range(channels // 128):
        gated[tile] = mixed[:, tile * 128 : (tile + 1) * 128]
    block = 64
    start = halo - taps // 2
    for tile in range(channels // 128):
        lanes = slice(tile * 128, tile * 128 + 128)
        for base in range(0, quarter, block):
            total = None
            for k in range(taps):
                part = gated[tile, base + k + start : base + k + start + block, :] * taps_ref[k : k + 1, lanes]
                total = part if total is None else total + part
            hidden_ref[base : base + block, lanes] = (total * jax.nn.sigmoid(total)).astype(BF16)


def half_kernel(after_ref, hidden_ref, out_w_ref, base_ref):
    channels = hidden_ref.shape[1]
    mine, _ = halves(channels)
    base_ref[...] = after_ref[...].astype(F32) + dot(hidden_ref[...], out_w_ref[:, mine])


def last_kernel(
    parts, info_ref, base_ref, hidden_ref, out_w_ref, frames_ref, bypass_ref, out_ref, tall, flat, sems
):
    quarter, channels = base_ref.shape
    rows = quarter // parts
    step = 4 * rows
    mine, _ = halves(channels)
    weights = out_w_ref[:, mine]
    length = info_ref[1:2, 0:1]
    row = lax.broadcasted_iota(jnp.int32, (step, 128), 0) + lax.axis_index("tm") * 4 * quarter
    copies = []
    for i in range(parts):
        part = slice(i * rows, (i + 1) * rows)
        span = slice(i * step, (i + 1) * step)
        stacked = base_ref[part, :] + dot(hidden_ref[part, :], weights)
        live = row + i * step < length
        for tile in range(channels // 128):
            lanes = slice(tile * 128, tile * 128 + 128)
            for j in range(4):
                tall[tile, pl.ds(i * step + j, rows, stride=4), :] = stacked[:, lanes]
            backdrop = frames_ref[span, lanes].astype(F32)
            result = backdrop + bypass_ref[:, lanes] * (tall[tile, span] - backdrop)
            flat[span, lanes] = jnp.where(live, result, 0.0).astype(BF16)
        window = pl.ds(i * step, step)
        copies.append(pltpu.make_async_copy(flat.at[window], out_ref.at[window], sems.at[i]))
        copies[-1].start()
    for copy in copies:
        copy.wait()


def shards(
    frames,
    lengths,
    down_weights,
    w_query,
    w_key,
    w_value,
    w_out,
    conv_in,
    conv_taps,
    conv_out,
    bypass,
):
    records, frame_count, channels = frames.shape
    quarter = frame_count // 4
    heads = w_query.shape[1] // QDIM
    keys_wide = w_query.shape[1]
    count = lax.axis_size("tm")
    halo = -(-(conv_taps.shape[0] // 2) // 16) * 16
    queries = -(-(quarter + 2 * halo) // 128) * 128
    frames = frames.reshape(frame_count, channels)
    swap = [(0, 1), (1, 0)]

    def ring(array, by):
        return lax.ppermute(array, "tm", [(i, (i + by) % count) for i in range(count)])

    def vmem(shape, dtype):
        return pltpu.VMEM(shape, dtype)

    reduced, info = call(
        functools.partial(down_kernel, 4),
        [vmem((quarter, channels), BF16), vmem((8, 128), jnp.int32)],
        [lengths, frames, down_weights],
        [SM, HB, HB],
        "down",
        [
            pltpu.VMEM((frame_count, channels), BF16),
            pltpu.VMEM((channels // 128, frame_count, 128), F32),
            pltpu.VMEM(down_weights.shape, F32),
            pltpu.SemaphoreType.DMA((5,)),
        ],
        flops=8 * frame_count * channels,
        moved=3 * frame_count * channels,
    )
    theirs = lax.ppermute(reduced, "head", swap)
    edge_rows = halo * 2 * channels // 128
    to_right, to_left = call(
        functools.partial(kv_kernel, halo),
        [vmem((kv_rows(quarter, heads * VDIM) + edge_rows, keys_wide), BF16)] * 2,
        [reduced, theirs, w_key, w_value.T],
        [VM] * 4,
        "keys_values",
        flops=4 * quarter * channels * (keys_wide + heads * VDIM),
        moved=8 * quarter * channels,
    )
    right = [to_right, ring(to_right, 1)]
    left = [to_left, ring(to_left, -1)]
    steps_right, steps_left = count // 2, (count - 1) // 2
    for step in range(2, steps_right + 1):
        right.append(ring(right[-1], 1))
    for step in range(2, steps_left + 1):
        left.append(ring(left[-1], -1))
    their_w_out = lax.ppermute(w_out, "head", swap)
    their_conv_out = lax.ppermute(conv_out, "head", swap)

    stages = [[(0, to_right), (-1, right[1]), (1, left[1])]]
    for step in range(2, steps_right + 1):
        stage = [(-step, right[step])]
        if step <= steps_left:
            stage.append((step, left[step]))
        stages.append(stage)
    score_flops = 2 * quarter * queries * heads * (128 + 64)

    first = stages[0]
    rows, q_t, top, total = call(
        functools.partial(open_kernel, heads, halo, [shift for shift, _ in first]),
        [
            vmem((queries, 2 * channels), BF16),
            vmem((keys_wide, queries), F32),
            vmem((8, queries), F32),
            vmem((heads * VDIM + 16, queries), F32),
        ],
        [info, reduced, theirs, w_query] + [array for _, array in first],
        [VM] * (4 + len(first)),
        "attend_first",
        [pltpu.VMEM((len(first) * quarter, queries), F32)],
        flops=score_flops * len(first),
        moved=quarter * queries * 4,
        exps=quarter * queries * heads * len(first),
    )
    for index, stage in enumerate(stages[1:]):
        last = index == len(stages) - 2
        outs = [vmem((8, queries), F32), vmem((heads * VDIM + 16, queries), F32)]
        if last:
            outs = [vmem((heads * VDIM, queries), BF16)]
        state = call(
            functools.partial(more_kernel, heads, [shift for shift, _ in stage], last),
            outs,
            [info, q_t, top, total] + [array for _, array in stage],
            [VM] * (4 + len(stage)),
            "attend_more",
            [pltpu.VMEM((len(stage) * quarter, queries), F32)],
            flops=score_flops * len(stage),
            moved=quarter * queries * 4,
            exps=quarter * queries * heads * len(stage),
        )
        if last:
            attended = state[0]
        else:
            top, total = state
    their_attended = lax.ppermute(attended, "head", swap)
    after, hidden = call(
        functools.partial(conv_kernel, halo),
        [vmem((quarter, channels), BF16), vmem((quarter, channels), BF16)],
        [
            info, rows, attended, their_attended, w_out, their_w_out,
            conv_in.reshape(2 * channels, 2 * channels), conv_taps,
        ],
        [VM] * 8,
        "gate_conv",
        [pltpu.VMEM((channels // 128, quarter + 2 * halo, 128), F32)],
        flops=2 * queries * 2 * channels * (96 + 2 * channels),
        moved=quarter * channels * 8,
    )
    their_hidden = lax.ppermute(hidden, "head", swap)
    (base,) = call(
        half_kernel,
        [vmem((quarter, channels), F32)],
        [after, hidden, conv_out],
        [VM] * 3,
        "half_out",
        flops=2 * quarter * channels * channels,
        moved=quarter * channels * 4,
    )
    (out,) = call(
        functools.partial(last_kernel, 4),
        [jax.ShapeDtypeStruct((frame_count, channels), BF16)],
        [info, base, their_hidden, their_conv_out, frames, bypass.reshape(1, channels)],
        [VM] * 6,
        "bypass",
        [
            pltpu.VMEM((channels // 128, frame_count, 128), F32),
            pltpu.VMEM((frame_count, channels), BF16),
            pltpu.SemaphoreType.DMA((4,)),
        ],
        out_specs=[HB],
        flops=2 * quarter * channels * channels,
        moved=frame_count * channels * 4,
    )
    return out.reshape(records, frame_count, channels)


def solution(mesh):
    in_specs = (
        P(("groups", "dp"), "tm", "head"),
        P(("groups", "dp")),
        P(None, "head"),
        P(None, "head"),
        P(None, "head"),
        P(None, "head"),
        P("head", None),
        P(None, None, "head"),
        P(None, "head"),
        P("head", None),
        P("head"),
    )
    out_specs = P(("groups", "dp"), "tm", "head")
    return jax.shard_map(shards, mesh=mesh, in_specs=in_specs, out_specs=out_specs, check_vma=False)
```

```python
import functools
import math

import jax
import jax.numpy as jnp
from jax import lax
from jax.experimental import pallas as pl
from jax.experimental.pallas import tpu as pltpu
from jax.sharding import PartitionSpec as P

QDIM = 32
VDIM = 12
NEG = -1e30
F32 = jnp.float32
BF16 = jnp.bfloat16
VM = pl.BlockSpec(memory_space=pltpu.VMEM)
HB = pl.BlockSpec(memory_space=pltpu.HBM)
SM = pl.BlockSpec(memory_space=pltpu.SMEM)
NT = (((1,), (1,)), ((), ()))
TN = (((0,), (0,)), ((), ()))


def placed(array, spec):
    if spec is SM:
        return array
    return pltpu.with_memory_space_constraint(array, pltpu.VMEM if spec is VM else pltpu.HBM)


def call(kernel, outs, operands, specs, name, scratch=(), out_specs=None, flops=0, moved=0, exps=0):
    out_specs = out_specs or [VM] * len(outs)
    operands = [placed(a, s) for a, s in zip(operands, specs)]
    return pl.pallas_call(
        kernel,
        out_shape=outs,
        in_specs=specs,
        out_specs=out_specs,
        scratch_shapes=list(scratch),
        name=name,
        compiler_params=pltpu.CompilerParams(vmem_limit_bytes=24 * 2**20),
        cost_estimate=pl.CostEstimate(flops=flops, bytes_accessed=moved, transcendentals=exps),
    )(*operands)


def dot(a, b, dims=None):
    if dims is None:
        return jnp.dot(a, b, preferred_element_type=F32)
    return lax.dot_general(a, b, dims, preferred_element_type=F32)


def halves(channels):
    here = lax.axis_index("head")
    mine = pl.ds(pl.multiple_of(here * channels, channels), channels)
    theirs = pl.ds(pl.multiple_of((1 - here) * channels, channels), channels)
    return mine, theirs


def down_kernel(parts, len_ref, frames_ref, weights_hbm, out_ref, info_ref, raw, wide, weights_ref, sems):
    frame_count, channels = raw.shape
    tiles = channels // 128
    step = frame_count // parts
    rows = step // 4
    copies = [
        pltpu.make_async_copy(
            frames_ref.at[pl.ds(i * step, step)], raw.at[pl.ds(i * step, step)], sems.at[i]
        )
        for i in range(parts)
    ]
    weights_copy = pltpu.make_async_copy(weights_hbm, weights_ref, sems.at[parts])
    weights_copy.start()
    for copy in copies:
        copy.start()
    length = len_ref[0]
    live_rows = lax.shift_right_logical(length + 3, 2)
    which = lax.broadcasted_iota(jnp.int32, info_ref.shape, 0)
    info_ref[...] = jnp.where(which == 0, live_rows, length)
    first = lax.axis_index("tm") * frame_count
    weights_copy.wait()
    for i in range(parts):
        copies[i].wait()
        base = first + i * step
        row = base + 4 * lax.broadcasted_iota(jnp.int32, (rows, 128), 0)
        for tile in range(tiles):
            lanes = slice(tile * 128, tile * 128 + 128)
            wide[tile, i * step : (i + 1) * step] = raw[i * step : (i + 1) * step, lanes].astype(F32)
            total = None
            for j in range(4):
                part = wide[tile, pl.ds(i * step + j, rows, stride=4), :]
                part = jnp.where(row + j < length, part, 0.0) * weights_ref[j : j + 1, lanes]
                total = part if total is None else total + part
            out_ref[i * rows : (i + 1) * rows, lanes] = total.astype(BF16)


def kv_rows(quarter, width):
    return quarter + width * ((quarter + 127) // 128)


def put_edge(pack_ref, at, halo, rows):
    for i in range(rows.shape[1] // 128):
        pack_ref[at + i * halo : at + (i + 1) * halo, :] = rows[:, i * 128 : (i + 1) * 128]
    return at + halo * (rows.shape[1] // 128)


def get_edge(pack_ref, at, halo, width):
    pieces = [pack_ref[at + i * halo : at + (i + 1) * halo, :] for i in range(width // 128)]
    return jnp.concatenate(pieces, axis=1)


def kv_kernel(halo, mine_ref, theirs_ref, wk_ref, wvt_ref, right_ref, left_ref):
    quarter, channels = mine_ref.shape
    width = wvt_ref.shape[0]
    mine, theirs = halves(channels)
    a, b = mine_ref[...], theirs_ref[...]
    keys = dot(a, wk_ref[mine, :]) + dot(b, wk_ref[theirs, :])
    keys = keys.astype(BF16)
    values_t = dot(wvt_ref[:, mine], a, NT) + dot(wvt_ref[:, theirs], b, NT)
    values_t = values_t.astype(BF16)
    for pack_ref, edge in ((right_ref, slice(quarter - halo, quarter)), (left_ref, slice(0, halo))):
        pack_ref[:quarter, :] = keys
        at = quarter
        for lane in range(0, quarter, 128):
            size = min(128, quarter - lane)
            if size < 128:
                pack_ref[at : at + width, :] = jnp.zeros((width, 128), BF16)
            pack_ref[at : at + width, :size] = values_t[:, lane : lane + size]
            at += width
        at = put_edge(pack_ref, at, halo, mine_ref[edge, :])
        put_edge(pack_ref, at, halo, theirs_ref[edge, :])


def head_query(q_t, head, ones):
    at = lax.broadcasted_iota(jnp.int32, q_t.shape, 0) // QDIM
    return jnp.concatenate([jnp.where(at == head, q_t, 0.0).astype(BF16), ones], axis=0)


def one_row(queries):
    at = lax.broadcasted_iota(jnp.int32, (128, queries), 0)
    return jnp.where(at == 0, 1.0, 0.0).astype(BF16)


def masked_keys(pack, quarter, first_row, live_rows):
    row = lax.broadcasted_iota(jnp.int32, (quarter, 128), 0) + first_row
    lane = lax.broadcasted_iota(jnp.int32, (quarter, 128), 1)
    bias = jnp.where((lane == 0) & (row >= live_rows), NEG, 0.0).astype(BF16)
    return jnp.concatenate([pack[:quarter, :], bias], axis=1)


def all_values(pack, quarter, width):
    pieces = []
    at = quarter
    for lane in range(0, quarter, 128):
        size = min(128, quarter - lane)
        pieces.append(pack[at : at + width, :size].astype(F32))
        at += width
    return jnp.concatenate(pieces, axis=1)


def head_values(values_t, head):
    width, quarter = values_t.shape
    row = lax.broadcasted_iota(jnp.int32, (width, quarter), 0)
    kept = jnp.where((row >= head * VDIM) & (row < (head + 1) * VDIM), values_t, 0.0).astype(BF16)
    extra = lax.broadcasted_iota(jnp.int32, (16, quarter), 0)
    ones = jnp.where(extra == head, 1.0, 0.0).astype(BF16)
    return jnp.concatenate([kept, ones], axis=0)


def spread(rows, shape, heads):
    at = lax.broadcasted_iota(jnp.int32, shape, 0)
    out = jnp.broadcast_to(rows[0], shape)
    for head in range(1, heads):
        ours = (at >= head * VDIM) & (at < (head + 1) * VDIM)
        out = jnp.where(ours, jnp.broadcast_to(rows[head], shape), out)
    return out


def absorb(total, q_t, packs, sources, live_rows, quarter, heads):
    ones = one_row(q_t.shape[1])
    for pack, source in zip(packs, sources):
        keys = masked_keys(pack, quarter, source * quarter, live_rows)
        values_t = all_values(pack, quarter, heads * VDIM)
        for head in range(heads):
            expo = jnp.exp2(dot(keys, head_query(q_t, head, ones))).astype(BF16)
            part = dot(head_values(values_t, head), expo)
            total = part if total is None else total + part
    return total


def finish(total, heads):
    width = heads * VDIM
    down = [total[width + head : width + head + 1, :] for head in range(heads)]
    return (total[:width, :] / spread(down, (width, total.shape[1]), heads)).astype(BF16)


def sources_of(shifts):
    here, count = lax.axis_index("tm"), lax.axis_size("tm")
    return [lax.rem(here + shift + count, count) for shift in shifts]


def open_kernel(heads, halo, shifts, info_ref, mine_ref, theirs_ref, wq_ref, *rest):
    packs = rest[: len(shifts)]
    rows_ref, qt_ref, sum_ref = rest[-3:]
    quarter, channels = mine_ref.shape
    edge = kv_rows(quarter, heads * VDIM)
    queries = rows_ref.shape[0]
    rows_ref[:halo, :] = get_edge(packs[1], edge, halo, 2 * channels)
    rows_ref[halo : halo + quarter, :channels] = mine_ref[...]
    rows_ref[halo : halo + quarter, channels:] = theirs_ref[...]
    rows_ref[halo + quarter : 2 * halo + quarter, :] = get_edge(packs[2], edge, halo, 2 * channels)
    rows_ref[2 * halo + quarter :, :] = jnp.zeros((queries - 2 * halo - quarter, 2 * channels), BF16)
    mine, theirs = halves(channels)
    query = dot(rows_ref[:, :channels], wq_ref[mine, :]) + dot(rows_ref[:, channels:], wq_ref[theirs, :])
    q_t = jnp.transpose(query * (math.log2(math.e) / math.sqrt(QDIM)))
    qt_ref[...] = q_t
    sum_ref[...] = absorb(None, q_t, packs, sources_of(shifts), info_ref[0:1, 0:1], quarter, heads)


def more_kernel(heads, quarter, shifts, info_ref, qt_ref, sum_in_ref, *rest):
    packs = rest[: len(shifts)]
    sum_ref = rest[-1]
    sum_ref[...] = absorb(
        sum_in_ref[...], qt_ref[...], packs, sources_of(shifts), info_ref[0:1, 0:1], quarter, heads
    )


def close_kernel(heads, quarter, shifts, everything, info_ref, qt_ref, sum_in_ref, *rest):
    packs = rest[: len(shifts) + len(everything)]
    out_ref, held, total_ref = rest[-3:]
    live_rows = info_ref[0:1, 0:1]
    width = heads * VDIM
    total = absorb(
        sum_in_ref[...], qt_ref[...], packs[: len(shifts)], sources_of(shifts), live_rows, quarter, heads
    )
    out_ref[...] = finish(total, heads)
    down = total[width : width + heads, :]
    safe = jnp.where((down > 2.0**-60) & (down < 2.0**100), 0.0, 1.0)

    @pl.when(jnp.max(safe) > 0.0)
    def _():
        count = lax.axis_size("tm")
        for i, (pack, shift) in enumerate(zip(packs, list(shifts) + list(everything))):
            held[i] = pack[...]
        firsts = sources_of(list(shifts) + list(everything))
        q_t = qt_ref[...]
        ones = one_row(q_t.shape[1])
        total_ref[...] = jnp.zeros_like(total_ref)

        def first_row(i):
            first = firsts[0]
            for j in range(1, count):
                first = jnp.where(i == j, firsts[j], first)
            return first * quarter

        def one_head(head, carry):
            query = head_query(q_t, head, ones)

            def scores(i):
                return dot(masked_keys(held.at[i], quarter, first_row(i), live_rows), query)

            def highest(i, top):
                return jnp.maximum(top, jnp.max(scores(i), axis=0, keepdims=True))

            top = lax.fori_loop(0, count, highest, jnp.full((1, q_t.shape[1]), NEG, F32))

            def add(i, carry):
                expo = jnp.exp2(scores(i) - top).astype(BF16)
                total_ref[...] += dot(head_values(all_values(held.at[i], quarter, width), head), expo)
                return carry

            return lax.fori_loop(0, count, add, carry)

        lax.fori_loop(0, heads, one_head, 0)
        out_ref[...] = finish(total_ref[...], heads)


def conv_kernel(
    halo, info_ref, rows_ref, mine_att_ref, their_att_ref, mine_out_ref, their_out_ref, conv_in_ref,
    taps_ref, after_ref, hidden_ref, gated,
):
    quarter, channels = hidden_ref.shape
    taps = taps_ref.shape[0]
    count = quarter + 2 * halo
    mine, theirs = halves(channels)
    attended = jnp.concatenate([mine_att_ref[...], their_att_ref[...]], axis=0)
    sides = []
    for side, lanes in ((mine, slice(0, channels)), (theirs, slice(channels, 2 * channels))):
        w_out = jnp.concatenate([mine_out_ref[:, side], their_out_ref[:, side]], axis=0)
        delta = dot(attended, w_out, TN)
        sides.append((rows_ref[:, lanes].astype(F32) + delta).astype(BF16)[:count])
    after_ref[...] = sides[0][halo : halo + quarter]
    gates = dot(sides[0], conv_in_ref[mine, :]) + dot(sides[1], conv_in_ref[theirs, :])
    value, gate = gates[:, :channels], gates[:, channels:]
    row = lax.broadcasted_iota(jnp.int32, (count, channels), 0)
    row = row + (lax.axis_index("tm") * quarter - halo)
    live = (row >= 0) & (row < info_ref[0:1, 0:1])
    mixed = jnp.where(live, value * jax.nn.sigmoid(gate), 0.0).astype(BF16).astype(F32)
    for tile in range(channels // 128):
        gated[tile] = mixed[:, tile * 128 : (tile + 1) * 128]
    block = 64
    start = halo - taps // 2
    for tile in range(channels // 128):
        lanes = slice(tile * 128, tile * 128 + 128)
        for base in range(0, quarter, block):
            total = None
            for k in range(taps):
                part = gated[tile, base + k + start : base + k + start + block, :] * taps_ref[k : k + 1, lanes]
                total = part if total is None else total + part
            hidden_ref[base : base + block, lanes] = (total * jax.nn.sigmoid(total)).astype(BF16)


def half_kernel(after_ref, hidden_ref, out_w_ref, base_ref):
    channels = hidden_ref.shape[1]
    mine, _ = halves(channels)
    base_ref[...] = after_ref[...].astype(F32) + dot(hidden_ref[...], out_w_ref[:, mine])


def last_kernel(
    parts, info_ref, base_ref, hidden_ref, out_w_ref, frames_ref, bypass_ref, out_ref, tall, flat, sems
):
    quarter, channels = base_ref.shape
    rows = quarter // parts
    step = 4 * rows
    mine, _ = halves(channels)
    weights = out_w_ref[:, mine]
    length = info_ref[1:2, 0:1]
    row = lax.broadcasted_iota(jnp.int32, (step, 128), 0) + lax.axis_index("tm") * 4 * quarter
    copies = []
    for i in range(parts):
        part = slice(i * rows, (i + 1) * rows)
        span = slice(i * step, (i + 1) * step)
        stacked = base_ref[part, :] + dot(hidden_ref[part, :], weights)
        live = row + i * step < length
        for tile in range(channels // 128):
            lanes = slice(tile * 128, tile * 128 + 128)
            for j in range(4):
                tall[tile, pl.ds(i * step + j, rows, stride=4), :] = stacked[:, lanes]
            backdrop = frames_ref[span, lanes].astype(F32)
            result = backdrop + bypass_ref[:, lanes] * (tall[tile, span] - backdrop)
            flat[span, lanes] = jnp.where(live, result, 0.0).astype(BF16)
        window = pl.ds(i * step, step)
        copies.append(pltpu.make_async_copy(flat.at[window], out_ref.at[window], sems.at[i]))
        copies[-1].start()
    for copy in copies:
        copy.wait()


def shards(
    frames,
    lengths,
    down_weights,
    w_query,
    w_key,
    w_value,
    w_out,
    conv_in,
    conv_taps,
    conv_out,
    bypass,
):
    records, frame_count, channels = frames.shape
    quarter = frame_count // 4
    heads = w_query.shape[1] // QDIM
    keys_wide = w_query.shape[1]
    count = lax.axis_size("tm")
    halo = -(-(conv_taps.shape[0] // 2) // 16) * 16
    queries = -(-(quarter + 2 * halo) // 128) * 128
    frames = frames.reshape(frame_count, channels)
    swap = [(0, 1), (1, 0)]

    def ring(array, by):
        return lax.ppermute(array, "tm", [(i, (i + by) % count) for i in range(count)])

    def vmem(shape, dtype):
        return pltpu.VMEM(shape, dtype)

    reduced, info, kept_frames = call(
        functools.partial(down_kernel, 4),
        [
            vmem((quarter, channels), BF16),
            vmem((8, 128), jnp.int32),
            vmem((frame_count, channels), BF16),
        ],
        [lengths, frames, down_weights],
        [SM, HB, HB],
        "down",
        [
            pltpu.VMEM((channels // 128, frame_count, 128), F32),
            pltpu.VMEM(down_weights.shape, F32),
            pltpu.SemaphoreType.DMA((5,)),
        ],
        flops=8 * frame_count * channels,
        moved=3 * frame_count * channels,
    )
    theirs = lax.ppermute(reduced, "head", swap)
    edge_rows = halo * 2 * channels // 128
    to_right, to_left = call(
        functools.partial(kv_kernel, halo),
        [vmem((kv_rows(quarter, heads * VDIM) + edge_rows, keys_wide), BF16)] * 2,
        [reduced, theirs, w_key, w_value.T],
        [VM] * 4,
        "keys_values",
        flops=4 * quarter * channels * (keys_wide + heads * VDIM),
        moved=8 * quarter * channels,
    )
    right = [to_right, ring(to_right, 1)]
    left = [to_left, ring(to_left, -1)]
    steps_right, steps_left = count // 2, (count - 1) // 2
    for step in range(2, steps_right + 1):
        right.append(ring(right[-1], 1))
    for step in range(2, steps_left + 1):
        left.append(ring(left[-1], -1))
    their_w_out = lax.ppermute(w_out, "head", swap)
    their_conv_out = lax.ppermute(conv_out, "head", swap)
    gate_weights = conv_in.reshape(2 * channels, 2 * channels)
    weights_row = bypass.reshape(1, channels)
    early = [their_w_out, their_conv_out, gate_weights, weights_row, conv_taps, w_out, conv_out]

    stages = [[(0, to_right), (-1, right[1]), (1, left[1])]]
    for step in range(2, steps_right + 1):
        stage = [(-step, right[step])]
        if step <= steps_left:
            stage.append((step, left[step]))
        stages.append(stage)
    score_flops = 2 * quarter * queries * heads * (128 + 64)

    first = stages[0]
    width = heads * VDIM
    rows, q_t, total = call(
        functools.partial(open_kernel, heads, halo, [shift for shift, _ in first]),
        [
            vmem((queries, 2 * channels), BF16),
            vmem((keys_wide, queries), F32),
            vmem((width + 16, queries), F32),
        ],
        [info, reduced, theirs, w_query] + [array for _, array in first] + early,
        [VM] * (4 + len(first) + len(early)),
        "attend_first",
        flops=score_flops * len(first),
        moved=quarter * queries * 4,
        exps=quarter * queries * heads * len(first),
    )
    for stage in stages[1:-1]:
        (total,) = call(
            functools.partial(more_kernel, heads, quarter, [shift for shift, _ in stage]),
            [vmem((width + 16, queries), F32)],
            [info, q_t, total] + [array for _, array in stage],
            [VM] * (3 + len(stage)),
            "attend_more",
            flops=score_flops * len(stage),
            moved=quarter * queries * 4,
            exps=quarter * queries * heads * len(stage),
        )
    stage = stages[-1]
    others = [pair for group in stages[:-1] for pair in group]
    (attended,) = call(
        functools.partial(
            close_kernel, heads, quarter, [shift for shift, _ in stage], [shift for shift, _ in others]
        ),
        [vmem((width, queries), BF16)],
        [info, q_t, total] + [array for _, array in stage + others],
        [VM] * (3 + count),
        "attend_last",
        [pltpu.VMEM((count,) + to_right.shape, BF16), pltpu.VMEM((width + 16, queries), F32)],
        flops=score_flops * len(stage),
        moved=quarter * queries * 4,
        exps=quarter * queries * heads * len(stage),
    )
    their_attended = lax.ppermute(attended, "head", swap)
    after, hidden = call(
        functools.partial(conv_kernel, halo),
        [vmem((quarter, channels), BF16), vmem((quarter, channels), BF16)],
        [
            info, rows, attended, their_attended, w_out, their_w_out,
            gate_weights, conv_taps,
        ],
        [VM] * 8,
        "gate_conv",
        [pltpu.VMEM((channels // 128, quarter + 2 * halo, 128), F32)],
        flops=2 * queries * 2 * channels * (96 + 2 * channels),
        moved=quarter * channels * 8,
    )
    their_hidden = lax.ppermute(hidden, "head", swap)
    (base,) = call(
        half_kernel,
        [vmem((quarter, channels), F32)],
        [after, hidden, conv_out],
        [VM] * 3,
        "half_out",
        flops=2 * quarter * channels * channels,
        moved=quarter * channels * 4,
    )
    (out,) = call(
        functools.partial(last_kernel, 4),
        [jax.ShapeDtypeStruct((frame_count, channels), BF16)],
        [info, base, their_hidden, their_conv_out, kept_frames, weights_row],
        [VM] * 6,
        "bypass",
        [
            pltpu.VMEM((channels // 128, frame_count, 128), F32),
            pltpu.VMEM((frame_count, channels), BF16),
            pltpu.SemaphoreType.DMA((4,)),
        ],
        out_specs=[HB],
        flops=2 * quarter * channels * channels,
        moved=frame_count * channels * 4,
    )
    return out.reshape(records, frame_count, channels)


def solution(mesh):
    in_specs = (
        P(("groups", "dp"), "tm", "head"),
        P(("groups", "dp")),
        P(None, "head"),
        P(None, "head"),
        P(None, "head"),
        P(None, "head"),
        P("head", None),
        P(None, None, "head"),
        P(None, "head"),
        P("head", None),
        P("head"),
    )
    out_specs = P(("groups", "dp"), "tm", "head")
    return jax.shard_map(shards, mesh=mesh, in_specs=in_specs, out_specs=out_specs, check_vma=False)
```

```python
import functools
import math

import jax
import jax.numpy as jnp
from jax import lax
from jax.experimental import pallas as pl
from jax.experimental.pallas import tpu as pltpu
from jax.sharding import PartitionSpec as P

QDIM = 32
VDIM = 12
NEG = -1e30
F32 = jnp.float32
BF16 = jnp.bfloat16
VM = pl.BlockSpec(memory_space=pltpu.VMEM)
HB = pl.BlockSpec(memory_space=pltpu.HBM)
SM = pl.BlockSpec(memory_space=pltpu.SMEM)
NT = (((1,), (1,)), ((), ()))
TN = (((0,), (0,)), ((), ()))


def placed(array, spec):
    if spec is SM:
        return array
    return pltpu.with_memory_space_constraint(array, pltpu.VMEM if spec is VM else pltpu.HBM)


def call(kernel, outs, operands, specs, scratch=(), out_specs=None, flops=0, moved=0, exps=0):
    out_specs = out_specs or [VM] * len(outs)
    operands = [placed(a, s) for a, s in zip(operands, specs)]
    return pl.pallas_call(
        kernel,
        out_shape=outs,
        in_specs=specs,
        out_specs=out_specs,
        scratch_shapes=list(scratch),
        compiler_params=pltpu.CompilerParams(vmem_limit_bytes=24 * 2**20),
        cost_estimate=pl.CostEstimate(flops=flops, bytes_accessed=moved, transcendentals=exps),
    )(*operands)


def dot(a, b, dims=None):
    if dims is None:
        return jnp.dot(a, b, preferred_element_type=F32)
    return lax.dot_general(a, b, dims, preferred_element_type=F32)


def halves(channels):
    here = lax.axis_index("head")
    mine = pl.ds(pl.multiple_of(here * channels, channels), channels)
    theirs = pl.ds(pl.multiple_of((1 - here) * channels, channels), channels)
    return mine, theirs


def down_kernel(parts, len_ref, frames_ref, weights_hbm, out_ref, info_ref, raw, wide, weights_ref, sems):
    frame_count, channels = raw.shape
    tiles = channels // 128
    step = frame_count // parts
    rows = step // 4
    copies = [
        pltpu.make_async_copy(
            frames_ref.at[pl.ds(i * step, step)], raw.at[pl.ds(i * step, step)], sems.at[i]
        )
        for i in range(parts)
    ]
    weights_copy = pltpu.make_async_copy(weights_hbm, weights_ref, sems.at[parts])
    weights_copy.start()
    for copy in copies:
        copy.start()
    length = len_ref[0]
    live_rows = lax.shift_right_logical(length + 3, 2)
    which = lax.broadcasted_iota(jnp.int32, info_ref.shape, 0)
    info_ref[...] = jnp.where(which == 0, live_rows, length)
    first = lax.axis_index("tm") * frame_count
    weights_copy.wait()
    for i in range(parts):
        copies[i].wait()
        base = first + i * step
        row = base + 4 * lax.broadcasted_iota(jnp.int32, (rows, 128), 0)
        for tile in range(tiles):
            lanes = slice(tile * 128, tile * 128 + 128)
            wide[tile, i * step : (i + 1) * step] = raw[i * step : (i + 1) * step, lanes].astype(F32)
            total = None
            for j in range(4):
                part = wide[tile, pl.ds(i * step + j, rows, stride=4), :]
                part = jnp.where(row + j < length, part, 0.0) * weights_ref[j : j + 1, lanes]
                total = part if total is None else total + part
            out_ref[i * rows : (i + 1) * rows, lanes] = total.astype(BF16)


def pack_plan(quarter, width):
    full, rest = divmod(quarter, 128)
    folded = 2 * rest == 128 and width % 16 == 0
    last = 0 if rest == 0 else (-(-width // 32) * 16 if folded else width)
    rows = quarter + full * width + last
    first = min(quarter, -(-rows // 32) * 16)
    return first, rows - first, folded


def put_edge(pack_ref, at, halo, rows):
    for i in range(rows.shape[1] // 128):
        pack_ref[at + i * halo : at + (i + 1) * halo, :] = rows[:, i * 128 : (i + 1) * 128]
    return at + halo * (rows.shape[1] // 128)


def get_edge(pack_ref, at, halo, width):
    pieces = [pack_ref[at + i * halo : at + (i + 1) * halo, :] for i in range(width // 128)]
    return jnp.concatenate(pieces, axis=1)


def kv_kernel(halo, mine_ref, theirs_ref, wk_ref, wvt_ref, first_ref, second_ref, left_ref, right_ref):
    quarter, channels = mine_ref.shape
    width = wvt_ref.shape[0]
    first, second, folded = pack_plan(quarter, width)
    mine, theirs = halves(channels)
    a, b = mine_ref[...], theirs_ref[...]
    keys = dot(a, wk_ref[mine, :]) + dot(b, wk_ref[theirs, :])
    keys = keys.astype(BF16)
    values_t = dot(wvt_ref[:, mine], a, NT) + dot(wvt_ref[:, theirs], b, NT)
    for pack_ref in (first_ref, left_ref):
        pack_ref[:first, :] = keys[:first, :]
    for pack_ref in (second_ref, right_ref):
        pack_ref[: quarter - first, :] = keys[first:, :]
        at = quarter - first
        for lane in range(0, quarter - 127, 128):
            pack_ref[at : at + width, :] = values_t[:, lane : lane + 128].astype(BF16)
            at += width
        if quarter % 128:
            tail = values_t[:, quarter - quarter % 128 :]
            if folded:
                tail = jnp.concatenate([tail[: width // 2, :], tail[width // 2 :, :]], axis=1)
            tail = jnp.concatenate([tail, jnp.zeros((second - at - tail.shape[0], tail.shape[1]), F32)], axis=0)
            if tail.shape[1] < 128:
                tail = jnp.concatenate([tail, jnp.zeros((tail.shape[0], 128 - tail.shape[1]), F32)], axis=1)
            pack_ref[at:second, :] = tail.astype(BF16)
    at = put_edge(right_ref, second, halo, mine_ref[quarter - halo :, :])
    put_edge(right_ref, at, halo, theirs_ref[quarter - halo :, :])
    at = put_edge(left_ref, first, halo, mine_ref[:halo, :])
    put_edge(left_ref, at, halo, theirs_ref[:halo, :])


def head_query(q_t, head):
    at = lax.broadcasted_iota(jnp.int32, q_t.shape, 0) // QDIM
    return jnp.where(at == head, q_t, 0.0).astype(BF16)


def all_keys(pack, first, quarter):
    return jnp.concatenate([pack[0][:first, :], pack[1][: quarter - first, :]], axis=0)


def all_values(ref, at, end, quarter, width):
    folded = pack_plan(quarter, width)[2]
    pieces = []
    for _ in range(0, quarter - 127, 128):
        pieces.append(ref[at : at + width, :].astype(F32))
        at += width
    rest = quarter % 128
    if rest:
        tail = ref[at:end, :].astype(F32)
        if folded:
            half = width // 2
            tail = jnp.concatenate([tail[:half, :rest], tail[:half, rest : 2 * rest]], axis=0)
        pieces.append(tail[:width, :rest])
    return jnp.concatenate(pieces, axis=1)


def head_values(values_t, head, live_keys):
    width, quarter = values_t.shape
    row = lax.broadcasted_iota(jnp.int32, (width, quarter), 0)
    kept = jnp.where((row >= head * VDIM) & (row < (head + 1) * VDIM), values_t, 0.0).astype(BF16)
    extra = lax.broadcasted_iota(jnp.int32, (16, quarter), 0)
    key = lax.broadcasted_iota(jnp.int32, (16, quarter), 1)
    ones = jnp.where((extra == head) & (key < live_keys), 1.0, 0.0).astype(BF16)
    return jnp.concatenate([kept, ones], axis=0)


def spread(rows, shape, heads):
    at = lax.broadcasted_iota(jnp.int32, shape, 0)
    out = jnp.broadcast_to(rows[0], shape)
    for head in range(1, heads):
        ours = (at >= head * VDIM) & (at < (head + 1) * VDIM)
        out = jnp.where(ours, jnp.broadcast_to(rows[head], shape), out)
    return out


def absorb(total, q_t, packs, sources, live_rows, quarter, heads):
    queries = q_t.shape[1]
    tiles = [slice(at, min(at + 512, queries)) for at in range(0, queries, 512)]
    totals = [None if total is None else total[:, tile] for tile in tiles]
    asked = [head_query(q_t, head) for head in range(heads)]
    units = []
    first, second, _ = pack_plan(quarter, heads * VDIM)
    for pack, source in zip(packs, sources):
        keys = all_keys(pack, first, quarter)
        values_t = all_values(pack[1], quarter - first, second, quarter, heads * VDIM)
        for head in range(heads):
            values = head_values(values_t, head, live_rows - source * quarter)
            units += [(keys, values, head, i) for i in range(len(tiles))]

    def scores(unit):
        keys, _, head, i = unit
        return dot(keys, asked[head][:, tiles[i]])

    ahead = scores(units[0])
    for at, (_, values, _, i) in enumerate(units):
        now = ahead
        if at + 1 < len(units):
            ahead = scores(units[at + 1])
        part = dot(values, jnp.exp2(now).astype(BF16))
        totals[i] = part if totals[i] is None else totals[i] + part
    return jnp.concatenate(totals, axis=1)


def finish(total, heads):
    width = heads * VDIM
    down = [total[width + head : width + head + 1, :] for head in range(heads)]
    return (total[:width, :] / spread(down, (width, total.shape[1]), heads)).astype(BF16)


def sources_of(shifts):
    here, count = lax.axis_index("tm"), lax.axis_size("tm")
    return [lax.rem(here + shift + count, count) for shift in shifts]


def pairs_of(refs):
    return list(zip(refs[::2], refs[1::2]))


def scaled_queries(mine_rows, their_rows, wq_ref, channels):
    mine, theirs = halves(channels)
    query = dot(mine_rows, wq_ref[mine, :]) + dot(their_rows, wq_ref[theirs, :])
    return jnp.transpose(query * (math.log2(math.e) / math.sqrt(QDIM)))


def own_kernel(heads, info_ref, mine_ref, theirs_ref, wq_ref, first_ref, second_ref, *rest):
    qt_ref, sum_ref = rest[-2:]
    quarter, channels = mine_ref.shape
    queries = qt_ref.shape[1]
    blank = jnp.zeros((queries - quarter, channels), BF16)
    q_t = scaled_queries(
        jnp.concatenate([mine_ref[...], blank], axis=0),
        jnp.concatenate([theirs_ref[...], blank], axis=0),
        wq_ref,
        channels,
    )
    qt_ref[...] = q_t
    total = absorb(
        None, q_t, [(first_ref, second_ref)], sources_of([0]), info_ref[0:1, 0:1], quarter, heads
    )
    lane = lax.broadcasted_iota(jnp.int32, total.shape, 1)
    sum_ref[...] = jnp.where(lane < quarter, total, 0.0)


def open_kernel(heads, halo, shifts, info_ref, mine_ref, theirs_ref, wq_ref, qt_in_ref, sum_in_ref, *rest):
    packs = pairs_of(rest[: 2 * len(shifts)])
    rows_ref, qt_ref, sum_ref = rest[-3:]
    quarter, channels = mine_ref.shape
    first, second, _ = pack_plan(quarter, heads * VDIM)
    queries = rows_ref.shape[0]
    late = quarter - quarter % 128
    rows_ref[:quarter, :channels] = mine_ref[...]
    rows_ref[:quarter, channels:] = theirs_ref[...]
    rows_ref[quarter : quarter + halo, :] = get_edge(packs[1][1], second, halo, 2 * channels)
    rows_ref[quarter + halo : quarter + 2 * halo, :] = get_edge(packs[2][0], first, halo, 2 * channels)
    rows_ref[quarter + 2 * halo :, :] = jnp.zeros((queries - 2 * halo - quarter, 2 * channels), BF16)
    q_late = scaled_queries(rows_ref[late:, :channels], rows_ref[late:, channels:], wq_ref, channels)
    q_t = jnp.concatenate([qt_in_ref[:, :late], q_late], axis=1)
    qt_ref[...] = q_t
    live_rows = info_ref[0:1, 0:1]
    sources = sources_of(shifts)
    total = absorb(sum_in_ref[...], q_t, packs[1:], sources[1:], live_rows, quarter, heads)
    edge = absorb(None, q_late, packs[:1], sources[:1], live_rows, quarter, heads)
    lane = lax.broadcasted_iota(jnp.int32, edge.shape, 1) + late
    edge = jnp.where(lane < quarter, 0.0, edge)
    sum_ref[:, :late] = total[:, :late]
    sum_ref[:, late:] = total[:, late:] + edge


def more_kernel(heads, quarter, shifts, info_ref, qt_ref, sum_in_ref, *rest):
    packs = pairs_of(rest[: 2 * len(shifts)])
    sum_ref = rest[-1]
    sum_ref[...] = absorb(
        sum_in_ref[...], qt_ref[...], packs, sources_of(shifts), info_ref[0:1, 0:1], quarter, heads
    )


def close_kernel(heads, quarter, shifts, everything, info_ref, qt_ref, sum_in_ref, *rest):
    packs = pairs_of(rest[: 2 * len(shifts) + 2 * len(everything)])
    out_ref, held, total_ref = rest[-3:]
    live_rows = info_ref[0:1, 0:1]
    width = heads * VDIM
    total = absorb(
        sum_in_ref[...], qt_ref[...], packs[: len(shifts)], sources_of(shifts), live_rows, quarter, heads
    )
    out_ref[...] = finish(total, heads)
    down = total[width : width + heads, :]
    safe = jnp.where((down > 2.0**-60) & (down < 2.0**100), 0.0, 1.0)

    @pl.when(jnp.max(safe) > 0.0)
    def _():
        count = lax.axis_size("tm")
        first, second, _ = pack_plan(quarter, width)
        for i, (pack, shift) in enumerate(zip(packs, list(shifts) + list(everything))):
            held[i, :first, :] = pack[0][:first, :]
            held[i, first:, :] = pack[1][:second, :]
        firsts = sources_of(list(shifts) + list(everything))
        q_t = qt_ref[...]
        row = lax.broadcasted_iota(jnp.int32, (quarter, q_t.shape[1]), 0)
        total_ref[...] = jnp.zeros_like(total_ref)

        def first_row(i):
            first = firsts[0]
            for j in range(1, count):
                first = jnp.where(i == j, firsts[j], first)
            return first * quarter

        def one_head(head, carry):
            query = head_query(q_t, head)

            def scores(i):
                return jnp.where(row < live_rows - first_row(i), dot(held[i, :quarter, :], query), NEG)

            def highest(i, top):
                return jnp.maximum(top, jnp.max(scores(i), axis=0, keepdims=True))

            top = lax.fori_loop(0, count, highest, jnp.full((1, q_t.shape[1]), NEG, F32))

            def add(i, carry):
                expo = jnp.exp2(scores(i) - top).astype(BF16)
                values = all_values(held.at[i], quarter, first + second, quarter, width)
                values = head_values(values, head, live_rows - first_row(i))
                total_ref[...] += dot(values, expo)
                return carry

            return lax.fori_loop(0, count, add, carry)

        lax.fori_loop(0, heads, one_head, 0)
        out_ref[...] = finish(total_ref[...], heads)


def conv_kernel(
    halo, info_ref, rows_ref, mine_att_ref, their_att_ref, mine_out_ref, their_out_ref, conv_in_ref,
    taps_ref, after_ref, hidden_ref, gated,
):
    quarter, channels = hidden_ref.shape
    taps = taps_ref.shape[0]
    count = quarter + 2 * halo
    mine, theirs = halves(channels)
    attended = jnp.concatenate([mine_att_ref[...], their_att_ref[...]], axis=0)
    sides = []
    for side, lanes in ((mine, slice(0, channels)), (theirs, slice(channels, 2 * channels))):
        w_out = jnp.concatenate([mine_out_ref[:, side], their_out_ref[:, side]], axis=0)
        delta = dot(attended, w_out, TN)
        sides.append((rows_ref[:, lanes].astype(F32) + delta).astype(BF16)[:count])
    after_ref[...] = sides[0][:quarter]
    gates = dot(sides[0], conv_in_ref[mine, :]) + dot(sides[1], conv_in_ref[theirs, :])
    value, gate = gates[:, :channels], gates[:, channels:]
    row = lax.broadcasted_iota(jnp.int32, (count, channels), 0)
    row = jnp.where((row >= quarter) & (row < quarter + halo), row - (quarter + halo), row)
    row = jnp.where(row >= quarter + halo, row - halo, row) + lax.axis_index("tm") * quarter
    live = (row >= 0) & (row < info_ref[0:1, 0:1])
    mixed = jnp.where(live, value * jax.nn.sigmoid(gate), 0.0).astype(BF16).astype(F32)
    for tile in range(channels // 128):
        lanes = slice(tile * 128, tile * 128 + 128)
        gated[tile, :halo] = mixed[quarter : quarter + halo, lanes]
        gated[tile, halo : halo + quarter] = mixed[:quarter, lanes]
        gated[tile, halo + quarter :] = mixed[quarter + halo :, lanes]
    block = 64
    start = halo - taps // 2
    for tile in range(channels // 128):
        lanes = slice(tile * 128, tile * 128 + 128)
        for base in range(0, quarter, block):
            total = None
            for k in range(taps):
                part = gated[tile, base + k + start : base + k + start + block, :] * taps_ref[k : k + 1, lanes]
                total = part if total is None else total + part
            hidden_ref[base : base + block, lanes] = (total * jax.nn.sigmoid(total)).astype(BF16)


def half_kernel(after_ref, hidden_ref, out_w_ref, bypass_hbm, base_ref, bypass_ref, sem):
    copy = pltpu.make_async_copy(bypass_hbm, bypass_ref, sem.at[0])
    copy.start()
    channels = hidden_ref.shape[1]
    mine, _ = halves(channels)
    base_ref[...] = after_ref[...].astype(F32) + dot(hidden_ref[...], out_w_ref[:, mine])
    copy.wait()


def last_kernel(
    parts, info_ref, base_ref, hidden_ref, out_w_ref, frames_ref, bypass_ref, out_ref, tall, flat, sems
):
    quarter, channels = base_ref.shape
    rows = quarter // parts
    step = 4 * rows
    mine, _ = halves(channels)
    weights = out_w_ref[:, mine]
    length = info_ref[1:2, 0:1]
    row = lax.broadcasted_iota(jnp.int32, (step, 128), 0) + lax.axis_index("tm") * 4 * quarter
    copies = []
    for i in range(parts):
        part = slice(i * rows, (i + 1) * rows)
        span = slice(i * step, (i + 1) * step)
        stacked = base_ref[part, :] + dot(hidden_ref[part, :], weights)
        live = row + i * step < length
        for tile in range(channels // 128):
            lanes = slice(tile * 128, tile * 128 + 128)
            for j in range(4):
                tall[tile, pl.ds(i * step + j, rows, stride=4), :] = stacked[:, lanes]
            backdrop = frames_ref[span, lanes].astype(F32)
            result = backdrop + bypass_ref[:, lanes] * (tall[tile, span] - backdrop)
            flat[span, lanes] = jnp.where(live, result, 0.0).astype(BF16)
        window = pl.ds(i * step, step)
        copies.append(pltpu.make_async_copy(flat.at[window], out_ref.at[window], sems.at[i]))
        copies[-1].start()
    for copy in copies:
        copy.wait()


def shards(
    frames,
    lengths,
    down_weights,
    w_query,
    w_key,
    w_value,
    w_out,
    conv_in,
    conv_taps,
    conv_out,
    bypass,
):
    records, frame_count, channels = frames.shape
    quarter = frame_count // 4
    heads = w_query.shape[1] // QDIM
    keys_wide = w_query.shape[1]
    count = lax.axis_size("tm")
    halo = -(-(conv_taps.shape[0] // 2) // 16) * 16
    queries = -(-(quarter + 2 * halo) // 128) * 128
    frames = frames.reshape(frame_count, channels)
    swap = [(0, 1), (1, 0)]

    def ring(array, by):
        return lax.ppermute(array, "tm", [(i, (i + by) % count) for i in range(count)])

    def vmem(shape, dtype):
        return pltpu.VMEM(shape, dtype)

    reduced, info, kept_frames = call(
        functools.partial(down_kernel, 4),
        [
            vmem((quarter, channels), BF16),
            vmem((8, 128), jnp.int32),
            vmem((frame_count, channels), BF16),
        ],
        [lengths, frames, down_weights],
        [SM, HB, HB],
        [
            pltpu.VMEM((channels // 128, frame_count, 128), F32),
            pltpu.VMEM(down_weights.shape, F32),
            pltpu.SemaphoreType.DMA((5,)),
        ],
        flops=8 * frame_count * channels,
        moved=3 * frame_count * channels,
    )
    theirs = lax.ppermute(reduced, "head", swap)
    width = heads * VDIM
    edge_rows = halo * 2 * channels // 128
    first_rows, second_rows, _ = pack_plan(quarter, width)
    first, second, first_left, second_right = call(
        functools.partial(kv_kernel, halo),
        [
            vmem((first_rows, keys_wide), BF16),
            vmem((second_rows, keys_wide), BF16),
            vmem((first_rows + edge_rows, keys_wide), BF16),
            vmem((second_rows + edge_rows, keys_wide), BF16),
        ],
        [reduced, theirs, w_key, w_value.T],
        [VM] * 4,
        flops=4 * quarter * channels * (keys_wide + width),
        moved=8 * quarter * channels,
    )
    reach = count // 2
    right_first, left_second = [ring(first, 1)], [ring(second, -1)]
    right_second, left_first = [ring(second_right, 1)], [ring(first_left, -1)]
    for step in range(2, reach + 1):
        right_first.append(ring(right_first[-1], 1))
        left_second.append(ring(left_second[-1], -1))
        if step < reach:
            right_second.append(ring(right_second[-1], 1))
            left_first.append(ring(left_first[-1], -1))
    their_w_out = lax.ppermute(w_out, "head", swap)
    their_conv_out = lax.ppermute(conv_out, "head", swap)
    gate_weights = conv_in.reshape(2 * channels, 2 * channels)
    early = [their_w_out, their_conv_out, gate_weights, conv_taps, w_out, conv_out]

    stages = [[(0, first, second), (-1, right_first[0], right_second[0]), (1, left_first[0], left_second[0])]]
    for step in range(2, reach):
        at = step - 1
        stages.append([(-step, right_first[at], right_second[at]), (step, left_first[at], left_second[at])])
    stages.append([(reach, right_first[-1], left_second[-1])])
    score_flops = 2 * quarter * queries * heads * (128 + 64)

    def arrays(stage):
        return [array for pack in stage for array in pack[1:]]

    def shifts(stage):
        return [pack[0] for pack in stage]

    q_t, total = call(
        functools.partial(own_kernel, heads),
        [vmem((keys_wide, queries), F32), vmem((width + 16, queries), F32)],
        [info, reduced, theirs, w_query, first, second] + early,
        [VM] * (6 + len(early)),
        flops=score_flops,
        moved=quarter * queries * 4,
        exps=quarter * queries * heads,
    )
    rows, q_t, total = call(
        functools.partial(open_kernel, heads, halo, shifts(stages[0])),
        [
            vmem((queries, 2 * channels), BF16),
            vmem((keys_wide, queries), F32),
            vmem((width + 16, queries), F32),
        ],
        [info, reduced, theirs, w_query, q_t, total] + arrays(stages[0]),
        [VM] * (6 + 2 * len(stages[0])),
        flops=score_flops * len(stages[0]),
        moved=quarter * queries * 4,
        exps=quarter * queries * heads * len(stages[0]),
    )
    for stage in stages[1:-1]:
        (total,) = call(
            functools.partial(more_kernel, heads, quarter, shifts(stage)),
            [vmem((width + 16, queries), F32)],
            [info, q_t, total] + arrays(stage),
            [VM] * (3 + 2 * len(stage)),
            flops=score_flops * len(stage),
            moved=quarter * queries * 4,
            exps=quarter * queries * heads * len(stage),
        )
    stage = stages[-1]
    others = [pack for group in stages[:-1] for pack in group]
    (attended,) = call(
        functools.partial(close_kernel, heads, quarter, shifts(stage), shifts(others)),
        [vmem((width, queries), BF16)],
        [info, q_t, total] + arrays(stage + others),
        [VM] * (3 + 2 * count),
        [
            pltpu.VMEM((count, first_rows + second_rows, keys_wide), BF16),
            pltpu.VMEM((width + 16, queries), F32),
        ],
        flops=score_flops * len(stage),
        moved=quarter * queries * 4,
        exps=quarter * queries * heads * len(stage),
    )
    their_attended = lax.ppermute(attended, "head", swap)
    after, hidden = call(
        functools.partial(conv_kernel, halo),
        [vmem((quarter, channels), BF16), vmem((quarter, channels), BF16)],
        [
            info, rows, attended, their_attended, w_out, their_w_out,
            gate_weights, conv_taps,
        ],
        [VM] * 8,
        [pltpu.VMEM((channels // 128, quarter + 2 * halo, 128), F32)],
        flops=2 * queries * 2 * channels * (96 + 2 * channels),
        moved=quarter * channels * 8,
    )
    their_hidden = lax.ppermute(hidden, "head", swap)
    base, kept_bypass = call(
        half_kernel,
        [vmem((quarter, channels), F32), vmem((1, channels), F32)],
        [after, hidden, conv_out, bypass.reshape(1, channels)],
        [VM, VM, VM, HB],
        [pltpu.SemaphoreType.DMA((1,))],
        flops=2 * quarter * channels * channels,
        moved=quarter * channels * 4,
    )
    (out,) = call(
        functools.partial(last_kernel, 4),
        [jax.ShapeDtypeStruct((frame_count, channels), BF16)],
        [info, base, their_hidden, their_conv_out, kept_frames, kept_bypass],
        [VM] * 6,
        [
            pltpu.VMEM((channels // 128, frame_count, 128), F32),
            pltpu.VMEM((frame_count, channels), BF16),
            pltpu.SemaphoreType.DMA((4,)),
        ],
        out_specs=[HB],
        flops=2 * quarter * channels * channels,
        moved=frame_count * channels * 4,
    )
    return out.reshape(records, frame_count, channels)


def solution(mesh):
    in_specs = (
        P(("groups", "dp"), "tm", "head"),
        P(("groups", "dp")),
        P(None, "head"),
        P(None, "head"),
        P(None, "head"),
        P(None, "head"),
        P("head", None),
        P(None, None, "head"),
        P(None, "head"),
        P("head", None),
        P("head"),
    )
    out_specs = P(("groups", "dp"), "tm", "head")
    return jax.shard_map(shards, mesh=mesh, in_specs=in_specs, out_specs=out_specs, check_vma=False)
```

```python
import functools
import math

import jax
import jax.numpy as jnp
from jax import lax
from jax.experimental import pallas as pl
from jax.experimental.pallas import tpu as pltpu
from jax.sharding import PartitionSpec as P

QDIM = 32
VDIM = 12
NEG = -1e30
F32 = jnp.float32
BF16 = jnp.bfloat16
VM = pl.BlockSpec(memory_space=pltpu.VMEM)
HB = pl.BlockSpec(memory_space=pltpu.HBM)
SM = pl.BlockSpec(memory_space=pltpu.SMEM)
NT = (((1,), (1,)), ((), ()))
TN = (((0,), (0,)), ((), ()))


def placed(array, spec):
    if spec is SM:
        return array
    return pltpu.with_memory_space_constraint(array, pltpu.VMEM if spec is VM else pltpu.HBM)


def call(kernel, outs, operands, specs, scratch=(), out_specs=None, flops=0, moved=0, exps=0):
    out_specs = out_specs or [VM] * len(outs)
    operands = [placed(a, s) for a, s in zip(operands, specs)]
    return pl.pallas_call(
        kernel,
        out_shape=outs,
        in_specs=specs,
        out_specs=out_specs,
        scratch_shapes=list(scratch),
        compiler_params=pltpu.CompilerParams(vmem_limit_bytes=24 * 2**20),
        cost_estimate=pl.CostEstimate(flops=flops, bytes_accessed=moved, transcendentals=exps),
    )(*operands)


def dot(a, b, dims=None):
    if dims is None:
        return jnp.dot(a, b, preferred_element_type=F32)
    return lax.dot_general(a, b, dims, preferred_element_type=F32)


def halves(channels):
    here = lax.axis_index("head")
    mine = pl.ds(pl.multiple_of(here * channels, channels), channels)
    theirs = pl.ds(pl.multiple_of((1 - here) * channels, channels), channels)
    return mine, theirs


def down_kernel(
    parts, len_ref, frames_ref, weights_hbm, key_hbm, value_hbm, query_hbm,
    out_ref, info_ref, raw, key_ref, value_ref, query_ref, wide, weights_ref, sems,
):
    frame_count, channels = raw.shape
    tiles = channels // 128
    step = frame_count // parts
    rows = step // 4
    copies = [
        pltpu.make_async_copy(
            frames_ref.at[pl.ds(i * step, step)], raw.at[pl.ds(i * step, step)], sems.at[i]
        )
        for i in range(parts)
    ]
    weights_copy = pltpu.make_async_copy(weights_hbm, weights_ref, sems.at[parts])
    weights_copy.start()
    for copy in copies:
        copy.start()
    later = [
        pltpu.make_async_copy(key_hbm, key_ref, sems.at[parts + 1]),
        pltpu.make_async_copy(value_hbm, value_ref, sems.at[parts + 2]),
        pltpu.make_async_copy(query_hbm, query_ref, sems.at[parts + 3]),
    ]
    for copy in later:
        copy.start()
    length = len_ref[0]
    live_rows = lax.shift_right_logical(length + 3, 2)
    which = lax.broadcasted_iota(jnp.int32, info_ref.shape, 0)
    info_ref[...] = jnp.where(which == 0, live_rows, length)
    first = lax.axis_index("tm") * frame_count
    weights_copy.wait()
    for i in range(parts):
        copies[i].wait()
        base = first + i * step
        row = base + 4 * lax.broadcasted_iota(jnp.int32, (rows, 128), 0)
        for tile in range(tiles):
            lanes = slice(tile * 128, tile * 128 + 128)
            wide[tile, i * step : (i + 1) * step] = raw[i * step : (i + 1) * step, lanes].astype(F32)
            total = None
            for j in range(4):
                part = wide[tile, pl.ds(i * step + j, rows, stride=4), :]
                part = jnp.where(row + j < length, part, 0.0) * weights_ref[j : j + 1, lanes]
                total = part if total is None else total + part
            out_ref[i * rows : (i + 1) * rows, lanes] = total.astype(BF16)
    for copy in later:
        copy.wait()


def pack_plan(quarter, width):
    full, rest = divmod(quarter, 128)
    folded = 2 * rest == 128 and width % 16 == 0
    last = 0 if rest == 0 else (-(-width // 32) * 16 if folded else width)
    rows = quarter + full * width + last
    first = min(quarter, -(-rows // 32) * 16)
    return first, rows - first, folded


def put_edge(pack_ref, at, halo, rows):
    for i in range(rows.shape[1] // 128):
        pack_ref[at + i * halo : at + (i + 1) * halo, :] = rows[:, i * 128 : (i + 1) * 128]
    return at + halo * (rows.shape[1] // 128)


def get_edge(pack_ref, at, halo, width):
    pieces = [pack_ref[at + i * halo : at + (i + 1) * halo, :] for i in range(width // 128)]
    return jnp.concatenate(pieces, axis=1)


def kv_kernel(halo, mine_ref, theirs_ref, wk_ref, wvt_ref, first_ref, second_ref, left_ref, right_ref):
    quarter, channels = mine_ref.shape
    width = wvt_ref.shape[0]
    first, second, folded = pack_plan(quarter, width)
    mine, theirs = halves(channels)
    a, b = mine_ref[...], theirs_ref[...]
    keys = dot(a, wk_ref[mine, :]) + dot(b, wk_ref[theirs, :])
    keys = keys.astype(BF16)
    values_t = dot(wvt_ref[:, mine], a, NT) + dot(wvt_ref[:, theirs], b, NT)
    for pack_ref in (first_ref, left_ref):
        pack_ref[:first, :] = keys[:first, :]
    for pack_ref in (second_ref, right_ref):
        pack_ref[: quarter - first, :] = keys[first:, :]
        at = quarter - first
        for lane in range(0, quarter - 127, 128):
            pack_ref[at : at + width, :] = values_t[:, lane : lane + 128].astype(BF16)
            at += width
        if quarter % 128:
            tail = values_t[:, quarter - quarter % 128 :]
            if folded:
                tail = jnp.concatenate([tail[: width // 2, :], tail[width // 2 :, :]], axis=1)
            tail = jnp.concatenate([tail, jnp.zeros((second - at - tail.shape[0], tail.shape[1]), F32)], axis=0)
            if tail.shape[1] < 128:
                tail = jnp.concatenate([tail, jnp.zeros((tail.shape[0], 128 - tail.shape[1]), F32)], axis=1)
            pack_ref[at:second, :] = tail.astype(BF16)
    at = put_edge(right_ref, second, halo, mine_ref[quarter - halo :, :])
    put_edge(right_ref, at, halo, theirs_ref[quarter - halo :, :])
    at = put_edge(left_ref, first, halo, mine_ref[:halo, :])
    put_edge(left_ref, at, halo, theirs_ref[:halo, :])


def head_query(q_t, head):
    at = lax.broadcasted_iota(jnp.int32, q_t.shape, 0) // QDIM
    return jnp.where(at == head, q_t, 0.0).astype(BF16)


def all_keys(pack, first, quarter):
    return jnp.concatenate([pack[0][:first, :], pack[1][: quarter - first, :]], axis=0)


def all_values(ref, at, end, quarter, width):
    folded = pack_plan(quarter, width)[2]
    pieces = []
    for _ in range(0, quarter - 127, 128):
        pieces.append(ref[at : at + width, :].astype(F32))
        at += width
    rest = quarter % 128
    if rest:
        tail = ref[at:end, :].astype(F32)
        if folded:
            half = width // 2
            tail = jnp.concatenate([tail[:half, :rest], tail[:half, rest : 2 * rest]], axis=0)
        pieces.append(tail[:width, :rest])
    return jnp.concatenate(pieces, axis=1)


def head_values(values_t, head, live_keys):
    width, quarter = values_t.shape
    row = lax.broadcasted_iota(jnp.int32, (width, quarter), 0)
    kept = jnp.where((row >= head * VDIM) & (row < (head + 1) * VDIM), values_t, 0.0).astype(BF16)
    extra = lax.broadcasted_iota(jnp.int32, (16, quarter), 0)
    key = lax.broadcasted_iota(jnp.int32, (16, quarter), 1)
    ones = jnp.where((extra == head) & (key < live_keys), 1.0, 0.0).astype(BF16)
    return jnp.concatenate([kept, ones], axis=0)


def spread(rows, shape, heads):
    at = lax.broadcasted_iota(jnp.int32, shape, 0)
    out = jnp.broadcast_to(rows[0], shape)
    for head in range(1, heads):
        ours = (at >= head * VDIM) & (at < (head + 1) * VDIM)
        out = jnp.where(ours, jnp.broadcast_to(rows[head], shape), out)
    return out


def absorb(total, q_t, packs, sources, live_rows, quarter, heads):
    queries = q_t.shape[1]
    tiles = [slice(at, min(at + 512, queries)) for at in range(0, queries, 512)]
    totals = [None if total is None else total[:, tile] for tile in tiles]
    asked = [head_query(q_t, head) for head in range(heads)]
    units = []
    first, second, _ = pack_plan(quarter, heads * VDIM)
    for pack, source in zip(packs, sources):
        keys = all_keys(pack, first, quarter)
        values_t = all_values(pack[1], quarter - first, second, quarter, heads * VDIM)
        for head in range(heads):
            values = head_values(values_t, head, live_rows - source * quarter)
            units += [(keys, values, head, i) for i in range(len(tiles))]

    def scores(unit):
        keys, _, head, i = unit
        return dot(keys, asked[head][:, tiles[i]])

    ahead = scores(units[0])
    for at, (_, values, _, i) in enumerate(units):
        now = ahead
        if at + 1 < len(units):
            ahead = scores(units[at + 1])
        part = dot(values, jnp.exp2(now).astype(BF16))
        totals[i] = part if totals[i] is None else totals[i] + part
    return jnp.concatenate(totals, axis=1)


def finish(total, heads):
    width = heads * VDIM
    down = [total[width + head : width + head + 1, :] for head in range(heads)]
    return (total[:width, :] / spread(down, (width, total.shape[1]), heads)).astype(BF16)


def sources_of(shifts):
    here, count = lax.axis_index("tm"), lax.axis_size("tm")
    return [lax.rem(here + shift + count, count) for shift in shifts]


def pairs_of(refs):
    return list(zip(refs[::2], refs[1::2]))


def scaled_queries(mine_rows, their_rows, wq_ref, channels):
    mine, theirs = halves(channels)
    query = dot(mine_rows, wq_ref[mine, :]) + dot(their_rows, wq_ref[theirs, :])
    return jnp.transpose(query * (math.log2(math.e) / math.sqrt(QDIM)))


def query_kernel(mine_ref, theirs_ref, wq_ref, qt_ref):
    quarter, channels = mine_ref.shape
    queries = qt_ref.shape[1]
    blank = jnp.zeros((queries - quarter, channels), BF16)
    qt_ref[...] = scaled_queries(
        jnp.concatenate([mine_ref[...], blank], axis=0),
        jnp.concatenate([theirs_ref[...], blank], axis=0),
        wq_ref,
        channels,
    )


def own_kernel(heads, quarter, info_ref, qt_ref, first_ref, second_ref, bypass_hbm, *rest):
    sum_ref, bypass_ref, sem = rest[-3:]
    copy = pltpu.make_async_copy(bypass_hbm, bypass_ref, sem.at[0])
    copy.start()
    total = absorb(
        None, qt_ref[...], [(first_ref, second_ref)], sources_of([0]), info_ref[0:1, 0:1], quarter, heads
    )
    lane = lax.broadcasted_iota(jnp.int32, total.shape, 1)
    sum_ref[...] = jnp.where(lane < quarter, total, 0.0)
    copy.wait()


def open_kernel(heads, halo, shifts, info_ref, mine_ref, theirs_ref, wq_ref, qt_in_ref, sum_in_ref, *rest):
    packs = pairs_of(rest[: 2 * len(shifts)])
    rows_ref, qt_ref, sum_ref = rest[-3:]
    quarter, channels = mine_ref.shape
    first, second, _ = pack_plan(quarter, heads * VDIM)
    queries = rows_ref.shape[0]
    late = quarter - quarter % 128
    rows_ref[:quarter, :channels] = mine_ref[...]
    rows_ref[:quarter, channels:] = theirs_ref[...]
    rows_ref[quarter : quarter + halo, :] = get_edge(packs[1][1], second, halo, 2 * channels)
    rows_ref[quarter + halo : quarter + 2 * halo, :] = get_edge(packs[2][0], first, halo, 2 * channels)
    rows_ref[quarter + 2 * halo :, :] = jnp.zeros((queries - 2 * halo - quarter, 2 * channels), BF16)
    q_late = scaled_queries(rows_ref[late:, :channels], rows_ref[late:, channels:], wq_ref, channels)
    q_t = jnp.concatenate([qt_in_ref[:, :late], q_late], axis=1)
    qt_ref[...] = q_t
    live_rows = info_ref[0:1, 0:1]
    sources = sources_of(shifts)
    total = absorb(sum_in_ref[...], q_t, packs[1:], sources[1:], live_rows, quarter, heads)
    edge = absorb(None, q_late, packs[:1], sources[:1], live_rows, quarter, heads)
    lane = lax.broadcasted_iota(jnp.int32, edge.shape, 1) + late
    edge = jnp.where(lane < quarter, 0.0, edge)
    sum_ref[:, :late] = total[:, :late]
    sum_ref[:, late:] = total[:, late:] + edge


def more_kernel(heads, quarter, shifts, info_ref, qt_ref, sum_in_ref, *rest):
    packs = pairs_of(rest[: 2 * len(shifts)])
    sum_ref = rest[-1]
    sum_ref[...] = absorb(
        sum_in_ref[...], qt_ref[...], packs, sources_of(shifts), info_ref[0:1, 0:1], quarter, heads
    )


def close_kernel(heads, quarter, shifts, everything, info_ref, qt_ref, sum_in_ref, *rest):
    packs = pairs_of(rest[: 2 * len(shifts) + 2 * len(everything)])
    out_ref, held, total_ref = rest[-3:]
    live_rows = info_ref[0:1, 0:1]
    width = heads * VDIM
    total = absorb(
        sum_in_ref[...], qt_ref[...], packs[: len(shifts)], sources_of(shifts), live_rows, quarter, heads
    )
    out_ref[...] = finish(total, heads)
    down = total[width : width + heads, :]
    safe = jnp.where((down > 2.0**-60) & (down < 2.0**100), 0.0, 1.0)

    @pl.when(jnp.max(safe) > 0.0)
    def _():
        count = lax.axis_size("tm")
        first, second, _ = pack_plan(quarter, width)
        for i, (pack, shift) in enumerate(zip(packs, list(shifts) + list(everything))):
            held[i, :first, :] = pack[0][:first, :]
            held[i, first:, :] = pack[1][:second, :]
        firsts = sources_of(list(shifts) + list(everything))
        q_t = qt_ref[...]
        row = lax.broadcasted_iota(jnp.int32, (quarter, q_t.shape[1]), 0)
        total_ref[...] = jnp.zeros_like(total_ref)

        def first_row(i):
            first = firsts[0]
            for j in range(1, count):
                first = jnp.where(i == j, firsts[j], first)
            return first * quarter

        def one_head(head, carry):
            query = head_query(q_t, head)

            def scores(i):
                return jnp.where(row < live_rows - first_row(i), dot(held[i, :quarter, :], query), NEG)

            def highest(i, top):
                return jnp.maximum(top, jnp.max(scores(i), axis=0, keepdims=True))

            top = lax.fori_loop(0, count, highest, jnp.full((1, q_t.shape[1]), NEG, F32))

            def add(i, carry):
                expo = jnp.exp2(scores(i) - top).astype(BF16)
                values = all_values(held.at[i], quarter, first + second, quarter, width)
                values = head_values(values, head, live_rows - first_row(i))
                total_ref[...] += dot(values, expo)
                return carry

            return lax.fori_loop(0, count, add, carry)

        lax.fori_loop(0, heads, one_head, 0)
        out_ref[...] = finish(total_ref[...], heads)


def conv_kernel(
    halo, info_ref, rows_ref, mine_att_ref, their_att_ref, mine_out_ref, their_out_ref, conv_in_ref,
    taps_ref, after_ref, hidden_ref, gated,
):
    quarter, channels = hidden_ref.shape
    taps = taps_ref.shape[0]
    count = quarter + 2 * halo
    mine, theirs = halves(channels)
    attended = jnp.concatenate([mine_att_ref[...], their_att_ref[...]], axis=0)
    sides = []
    for side, lanes in ((mine, slice(0, channels)), (theirs, slice(channels, 2 * channels))):
        w_out = jnp.concatenate([mine_out_ref[:, side], their_out_ref[:, side]], axis=0)
        delta = dot(attended, w_out, TN)
        sides.append((rows_ref[:, lanes].astype(F32) + delta).astype(BF16)[:count])
    after_ref[...] = sides[0][:quarter]
    gates = dot(sides[0], conv_in_ref[mine, :]) + dot(sides[1], conv_in_ref[theirs, :])
    value, gate = gates[:, :channels], gates[:, channels:]
    row = lax.broadcasted_iota(jnp.int32, (count, channels), 0)
    row = jnp.where((row >= quarter) & (row < quarter + halo), row - (quarter + halo), row)
    row = jnp.where(row >= quarter + halo, row - halo, row) + lax.axis_index("tm") * quarter
    live = (row >= 0) & (row < info_ref[0:1, 0:1])
    mixed = jnp.where(live, value * jax.nn.sigmoid(gate), 0.0).astype(BF16).astype(F32)
    for tile in range(channels // 128):
        lanes = slice(tile * 128, tile * 128 + 128)
        gated[tile, :halo] = mixed[quarter : quarter + halo, lanes]
        gated[tile, halo : halo + quarter] = mixed[:quarter, lanes]
        gated[tile, halo + quarter :] = mixed[quarter + halo :, lanes]
    block = 64
    start = halo - taps // 2
    for tile in range(channels // 128):
        lanes = slice(tile * 128, tile * 128 + 128)
        for base in range(0, quarter, block):
            total = None
            for k in range(taps):
                part = gated[tile, base + k + start : base + k + start + block, :] * taps_ref[k : k + 1, lanes]
                total = part if total is None else total + part
            hidden_ref[base : base + block, lanes] = (total * jax.nn.sigmoid(total)).astype(BF16)


def half_kernel(info_ref, after_ref, hidden_ref, out_w_ref, frames_ref, bypass_ref, base_ref, kept_ref):
    quarter, channels = hidden_ref.shape
    mine, _ = halves(channels)
    base_ref[...] = after_ref[...].astype(F32) + dot(hidden_ref[...], out_w_ref[:, mine])
    row = lax.broadcasted_iota(jnp.int32, (4 * quarter, 128), 0) + lax.axis_index("tm") * 4 * quarter
    live = row < info_ref[1:2, 0:1]
    for tile in range(channels // 128):
        lanes = slice(tile * 128, tile * 128 + 128)
        backdrop = frames_ref[:, lanes].astype(F32)
        kept_ref[tile] = jnp.where(live, backdrop - bypass_ref[:, lanes] * backdrop, 0.0)


def last_kernel(
    parts, info_ref, base_ref, hidden_ref, out_w_ref, kept_ref, bypass_ref, out_ref, tall, flat, sems
):
    quarter, channels = base_ref.shape
    rows = quarter // parts
    step = 4 * rows
    mine, _ = halves(channels)
    weights = out_w_ref[:, mine]
    length = info_ref[1:2, 0:1]
    row = lax.broadcasted_iota(jnp.int32, (step, 128), 0) + lax.axis_index("tm") * 4 * quarter
    copies = []
    for i in range(parts):
        part = slice(i * rows, (i + 1) * rows)
        span = slice(i * step, (i + 1) * step)
        stacked = bypass_ref[...] * (base_ref[part, :] + dot(hidden_ref[part, :], weights))
        live = row < length - i * step
        for tile in range(channels // 128):
            lanes = slice(tile * 128, tile * 128 + 128)
            for j in range(4):
                tall[tile, pl.ds(i * step + j, rows, stride=4), :] = stacked[:, lanes]
            added = jnp.where(live, tall[tile, span], 0.0)
            flat[span, lanes] = (kept_ref[tile, span] + added).astype(BF16)
        window = pl.ds(i * step, step)
        copies.append(pltpu.make_async_copy(flat.at[window], out_ref.at[window], sems.at[i]))
        copies[-1].start()
    for copy in copies:
        copy.wait()


def shards(
    frames,
    lengths,
    down_weights,
    w_query,
    w_key,
    w_value,
    w_out,
    conv_in,
    conv_taps,
    conv_out,
    bypass,
):
    records, frame_count, channels = frames.shape
    quarter = frame_count // 4
    heads = w_query.shape[1] // QDIM
    keys_wide = w_query.shape[1]
    count = lax.axis_size("tm")
    halo = -(-(conv_taps.shape[0] // 2) // 16) * 16
    queries = -(-(quarter + 2 * halo) // 128) * 128
    parts = quarter // 64
    frames = frames.reshape(frame_count, channels)
    swap = [(0, 1), (1, 0)]

    def ring(array, by):
        return lax.ppermute(array, "tm", [(i, (i + by) % count) for i in range(count)])

    def vmem(shape, dtype):
        return pltpu.VMEM(shape, dtype)

    reduced, info, kept_frames, kept_key, kept_value, kept_query = call(
        functools.partial(down_kernel, parts),
        [
            vmem((quarter, channels), BF16),
            vmem((8, 128), jnp.int32),
            vmem((frame_count, channels), BF16),
            vmem(w_key.shape, BF16),
            vmem(w_value.shape[::-1], BF16),
            vmem(w_query.shape, BF16),
        ],
        [lengths, frames, down_weights, w_key, w_value.T, w_query],
        [SM, HB, HB, HB, HB, HB],
        [
            pltpu.VMEM((channels // 128, frame_count, 128), F32),
            pltpu.VMEM(down_weights.shape, F32),
            pltpu.SemaphoreType.DMA((parts + 4,)),
        ],
        flops=8 * frame_count * channels,
        moved=3 * frame_count * channels,
    )
    theirs = lax.ppermute(reduced, "head", swap)
    width = heads * VDIM
    edge_rows = halo * 2 * channels // 128
    first_rows, second_rows, _ = pack_plan(quarter, width)
    first, second, first_left, second_right = call(
        functools.partial(kv_kernel, halo),
        [
            vmem((first_rows, keys_wide), BF16),
            vmem((second_rows, keys_wide), BF16),
            vmem((first_rows + edge_rows, keys_wide), BF16),
            vmem((second_rows + edge_rows, keys_wide), BF16),
        ],
        [reduced, theirs, kept_key, kept_value],
        [VM] * 4,
        flops=4 * quarter * channels * (keys_wide + width),
        moved=8 * quarter * channels,
    )
    reach = count // 2
    right_first, left_second = [ring(first, 1)], [ring(second, -1)]
    right_second, left_first = [ring(second_right, 1)], [ring(first_left, -1)]
    for step in range(2, reach + 1):
        right_first.append(ring(right_first[-1], 1))
        left_second.append(ring(left_second[-1], -1))
        if step < reach:
            right_second.append(ring(right_second[-1], 1))
            left_first.append(ring(left_first[-1], -1))
    their_w_out = lax.ppermute(w_out, "head", swap)
    their_conv_out = lax.ppermute(conv_out, "head", swap)
    gate_weights = conv_in.reshape(2 * channels, 2 * channels)
    early = [their_w_out, their_conv_out, gate_weights, conv_taps, w_out, conv_out]

    stages = [[(0, first, second), (-1, right_first[0], right_second[0]), (1, left_first[0], left_second[0])]]
    for step in range(2, reach):
        at = step - 1
        stages.append([(-step, right_first[at], right_second[at]), (step, left_first[at], left_second[at])])
    stages.append([(reach, right_first[-1], left_second[-1])])
    score_flops = 2 * quarter * queries * heads * (128 + 64)

    def arrays(stage):
        return [array for pack in stage for array in pack[1:]]

    def shifts(stage):
        return [pack[0] for pack in stage]

    (q_t,) = call(
        query_kernel,
        [vmem((keys_wide, queries), F32)],
        [reduced, theirs, kept_query],
        [VM] * 3,
        flops=4 * quarter * channels * keys_wide,
        moved=4 * quarter * channels,
    )
    total, bypass_row = call(
        functools.partial(own_kernel, heads, quarter),
        [vmem((width + 16, queries), F32), vmem((1, channels), F32)],
        [info, q_t, first, second, bypass.reshape(1, channels)] + early,
        [VM] * 4 + [HB] + [VM] * len(early),
        [pltpu.SemaphoreType.DMA((1,))],
        flops=score_flops,
        moved=quarter * queries * 4,
        exps=quarter * queries * heads,
    )
    rows, q_t, total = call(
        functools.partial(open_kernel, heads, halo, shifts(stages[0])),
        [
            vmem((queries, 2 * channels), BF16),
            vmem((keys_wide, queries), F32),
            vmem((width + 16, queries), F32),
        ],
        [info, reduced, theirs, kept_query, q_t, total] + arrays(stages[0]),
        [VM] * (6 + 2 * len(stages[0])),
        flops=score_flops * len(stages[0]),
        moved=quarter * queries * 4,
        exps=quarter * queries * heads * len(stages[0]),
    )
    for stage in stages[1:-1]:
        (total,) = call(
            functools.partial(more_kernel, heads, quarter, shifts(stage)),
            [vmem((width + 16, queries), F32)],
            [info, q_t, total] + arrays(stage),
            [VM] * (3 + 2 * len(stage)),
            flops=score_flops * len(stage),
            moved=quarter * queries * 4,
            exps=quarter * queries * heads * len(stage),
        )
    stage = stages[-1]
    others = [pack for group in stages[:-1] for pack in group]
    (attended,) = call(
        functools.partial(close_kernel, heads, quarter, shifts(stage), shifts(others)),
        [vmem((width, queries), BF16)],
        [info, q_t, total] + arrays(stage + others),
        [VM] * (3 + 2 * count),
        [
            pltpu.VMEM((count, first_rows + second_rows, keys_wide), BF16),
            pltpu.VMEM((width + 16, queries), F32),
        ],
        flops=score_flops * len(stage),
        moved=quarter * queries * 4,
        exps=quarter * queries * heads * len(stage),
    )
    their_attended = lax.ppermute(attended, "head", swap)
    after, hidden = call(
        functools.partial(conv_kernel, halo),
        [vmem((quarter, channels), BF16), vmem((quarter, channels), BF16)],
        [
            info, rows, attended, their_attended, w_out, their_w_out,
            gate_weights, conv_taps,
        ],
        [VM] * 8,
        [pltpu.VMEM((channels // 128, quarter + 2 * halo, 128), F32)],
        flops=2 * queries * 2 * channels * (96 + 2 * channels),
        moved=quarter * channels * 8,
    )
    their_hidden = lax.ppermute(hidden, "head", swap)
    base, kept = call(
        half_kernel,
        [vmem((quarter, channels), F32), vmem((channels // 128, frame_count, 128), F32)],
        [info, after, hidden, conv_out, kept_frames, bypass_row],
        [VM] * 6,
        flops=2 * quarter * channels * channels,
        moved=quarter * channels * 4,
    )
    (out,) = call(
        functools.partial(last_kernel, parts),
        [jax.ShapeDtypeStruct((frame_count, channels), BF16)],
        [info, base, their_hidden, their_conv_out, kept, bypass_row],
        [VM] * 6,
        [
            pltpu.VMEM((channels // 128, frame_count, 128), F32),
            pltpu.VMEM((frame_count, channels), BF16),
            pltpu.SemaphoreType.DMA((parts,)),
        ],
        out_specs=[HB],
        flops=2 * quarter * channels * channels,
        moved=frame_count * channels * 4,
    )
    return out.reshape(records, frame_count, channels)


def solution(mesh):
    in_specs = (
        P(("groups", "dp"), "tm", "head"),
        P(("groups", "dp")),
        P(None, "head"),
        P(None, "head"),
        P(None, "head"),
        P(None, "head"),
        P("head", None),
        P(None, None, "head"),
        P(None, "head"),
        P("head", None),
        P("head"),
    )
    out_specs = P(("groups", "dp"), "tm", "head")
    return jax.shard_map(shards, mesh=mesh, in_specs=in_specs, out_specs=out_specs, check_vma=False)
```

```python
import functools
import math

import jax
import jax.numpy as jnp
from jax import lax
from jax.experimental import pallas as pl
from jax.experimental.pallas import tpu as pltpu
from jax.sharding import PartitionSpec as P

QDIM = 32
VDIM = 12
NEG = -1e30
F32 = jnp.float32
BF16 = jnp.bfloat16
VM = pl.BlockSpec(memory_space=pltpu.VMEM)
HB = pl.BlockSpec(memory_space=pltpu.HBM)
SM = pl.BlockSpec(memory_space=pltpu.SMEM)
NT = (((1,), (1,)), ((), ()))
TN = (((0,), (0,)), ((), ()))


def placed(array, spec):
    if spec is SM:
        return array
    return pltpu.with_memory_space_constraint(array, pltpu.VMEM if spec is VM else pltpu.HBM)


def call(kernel, outs, operands, specs, scratch=(), out_specs=None, flops=0, moved=0, exps=0):
    out_specs = out_specs or [VM] * len(outs)
    operands = [placed(a, s) for a, s in zip(operands, specs)]
    return pl.pallas_call(
        kernel,
        out_shape=outs,
        in_specs=specs,
        out_specs=out_specs,
        scratch_shapes=list(scratch),
        compiler_params=pltpu.CompilerParams(vmem_limit_bytes=24 * 2**20),
        cost_estimate=pl.CostEstimate(flops=flops, bytes_accessed=moved, transcendentals=exps),
    )(*operands)


def dot(a, b, dims=None):
    if dims is None:
        return jnp.dot(a, b, preferred_element_type=F32)
    return lax.dot_general(a, b, dims, preferred_element_type=F32)


def halves(channels):
    here = lax.axis_index("head")
    mine = pl.ds(pl.multiple_of(here * channels, channels), channels)
    theirs = pl.ds(pl.multiple_of((1 - here) * channels, channels), channels)
    return mine, theirs


def down_kernel(
    parts, len_ref, frames_ref, weights_hbm, key_hbm, value_hbm, query_hbm,
    out_ref, info_ref, raw, key_ref, value_ref, query_ref, wide, weights_ref, sems,
):
    frame_count, channels = raw.shape
    tiles = channels // 128
    step = frame_count // parts
    rows = step // 4
    copies = [
        pltpu.make_async_copy(
            frames_ref.at[pl.ds(i * step, step)], raw.at[pl.ds(i * step, step)], sems.at[i]
        )
        for i in range(parts)
    ]
    weights_copy = pltpu.make_async_copy(weights_hbm, weights_ref, sems.at[parts])
    weights_copy.start()
    for copy in copies:
        copy.start()
    later = [
        pltpu.make_async_copy(key_hbm, key_ref, sems.at[parts + 1]),
        pltpu.make_async_copy(value_hbm, value_ref, sems.at[parts + 2]),
        pltpu.make_async_copy(query_hbm, query_ref, sems.at[parts + 3]),
    ]
    for copy in later:
        copy.start()
    length = len_ref[0]
    live_rows = lax.shift_right_logical(length + 3, 2)
    which = lax.broadcasted_iota(jnp.int32, info_ref.shape, 0)
    info_ref[...] = jnp.where(which == 0, live_rows, length)
    first = lax.axis_index("tm") * frame_count
    weights_copy.wait()
    for i in range(parts):
        copies[i].wait()
        base = first + i * step
        row = base + 4 * lax.broadcasted_iota(jnp.int32, (rows, 128), 0)
        for tile in range(tiles):
            lanes = slice(tile * 128, tile * 128 + 128)
            wide[tile, i * step : (i + 1) * step] = raw[i * step : (i + 1) * step, lanes].astype(F32)
            total = None
            for j in range(4):
                part = wide[tile, pl.ds(i * step + j, rows, stride=4), :]
                part = jnp.where(row + j < length, part, 0.0) * weights_ref[j : j + 1, lanes]
                total = part if total is None else total + part
            out_ref[i * rows : (i + 1) * rows, lanes] = total.astype(BF16)
    for copy in later:
        copy.wait()


def pack_plan(quarter, width):
    full, rest = divmod(quarter, 128)
    folded = 2 * rest == 128 and width % 16 == 0
    last = 0 if rest == 0 else (-(-width // 32) * 16 if folded else width)
    rows = quarter + full * width + last
    first = min(quarter, -(-rows // 32) * 16)
    return first, rows - first, folded


def put_edge(pack_ref, at, halo, rows):
    for i in range(rows.shape[1] // 128):
        pack_ref[at + i * halo : at + (i + 1) * halo, :] = rows[:, i * 128 : (i + 1) * 128]
    return at + halo * (rows.shape[1] // 128)


def get_edge(pack_ref, at, halo, width):
    pieces = [pack_ref[at + i * halo : at + (i + 1) * halo, :] for i in range(width // 128)]
    return jnp.concatenate(pieces, axis=1)


def kv_kernel(halo, mine_ref, theirs_ref, wk_ref, wvt_ref, first_ref, second_ref, left_ref, right_ref):
    quarter, channels = mine_ref.shape
    width = wvt_ref.shape[0]
    first, second, folded = pack_plan(quarter, width)
    mine, theirs = halves(channels)
    a, b = mine_ref[...], theirs_ref[...]
    keys = dot(a, wk_ref[mine, :]) + dot(b, wk_ref[theirs, :])
    keys = keys.astype(BF16)
    values_t = dot(wvt_ref[:, mine], a, NT) + dot(wvt_ref[:, theirs], b, NT)
    for pack_ref in (first_ref, left_ref):
        pack_ref[:first, :] = keys[:first, :]
    for pack_ref in (second_ref, right_ref):
        pack_ref[: quarter - first, :] = keys[first:, :]
        at = quarter - first
        for lane in range(0, quarter - 127, 128):
            pack_ref[at : at + width, :] = values_t[:, lane : lane + 128].astype(BF16)
            at += width
        if quarter % 128:
            tail = values_t[:, quarter - quarter % 128 :]
            if folded:
                tail = jnp.concatenate([tail[: width // 2, :], tail[width // 2 :, :]], axis=1)
            tail = jnp.concatenate([tail, jnp.zeros((second - at - tail.shape[0], tail.shape[1]), F32)], axis=0)
            if tail.shape[1] < 128:
                tail = jnp.concatenate([tail, jnp.zeros((tail.shape[0], 128 - tail.shape[1]), F32)], axis=1)
            pack_ref[at:second, :] = tail.astype(BF16)
    at = put_edge(right_ref, second, halo, mine_ref[quarter - halo :, :])
    put_edge(right_ref, at, halo, theirs_ref[quarter - halo :, :])
    at = put_edge(left_ref, first, halo, mine_ref[:halo, :])
    put_edge(left_ref, at, halo, theirs_ref[:halo, :])


def head_query(q_t, head):
    at = lax.broadcasted_iota(jnp.int32, q_t.shape, 0) // QDIM
    return jnp.where(at == head, q_t, 0.0).astype(BF16)


def all_keys(pack, first, quarter):
    return jnp.concatenate([pack[0][:first, :], pack[1][: quarter - first, :]], axis=0)


def all_values(ref, at, end, quarter, width):
    folded = pack_plan(quarter, width)[2]
    pieces = []
    for _ in range(0, quarter - 127, 128):
        pieces.append(ref[at : at + width, :].astype(F32))
        at += width
    rest = quarter % 128
    if rest:
        tail = ref[at:end, :].astype(F32)
        if folded:
            half = width // 2
            tail = jnp.concatenate([tail[:half, :rest], tail[:half, rest : 2 * rest]], axis=0)
        pieces.append(tail[:width, :rest])
    return jnp.concatenate(pieces, axis=1)


def head_values(values_t, head, live_keys):
    width, quarter = values_t.shape
    row = lax.broadcasted_iota(jnp.int32, (width, quarter), 0)
    kept = jnp.where((row >= head * VDIM) & (row < (head + 1) * VDIM), values_t, 0.0).astype(BF16)
    extra = lax.broadcasted_iota(jnp.int32, (16, quarter), 0)
    key = lax.broadcasted_iota(jnp.int32, (16, quarter), 1)
    ones = jnp.where((extra == head) & (key < live_keys), 1.0, 0.0).astype(BF16)
    return jnp.concatenate([kept, ones], axis=0)


def spread(rows, shape, heads):
    at = lax.broadcasted_iota(jnp.int32, shape, 0)
    out = jnp.broadcast_to(rows[0], shape)
    for head in range(1, heads):
        ours = (at >= head * VDIM) & (at < (head + 1) * VDIM)
        out = jnp.where(ours, jnp.broadcast_to(rows[head], shape), out)
    return out


def absorb(total, q_t, packs, sources, live_rows, quarter, heads):
    queries = q_t.shape[1]
    tiles = [slice(at, min(at + 512, queries)) for at in range(0, queries, 512)]
    totals = [None if total is None else total[:, tile] for tile in tiles]
    asked = [head_query(q_t, head) for head in range(heads)]
    units = []
    first, second, _ = pack_plan(quarter, heads * VDIM)
    for pack, source in zip(packs, sources):
        keys = all_keys(pack, first, quarter)
        values_t = all_values(pack[1], quarter - first, second, quarter, heads * VDIM)
        for head in range(heads):
            values = head_values(values_t, head, live_rows - source * quarter)
            units += [(keys, values, head, i) for i in range(len(tiles))]

    def scores(unit):
        keys, _, head, i = unit
        return dot(keys, asked[head][:, tiles[i]])

    ahead = scores(units[0])
    for at, (_, values, _, i) in enumerate(units):
        now = ahead
        if at + 1 < len(units):
            ahead = scores(units[at + 1])
        part = dot(values, jnp.exp2(now).astype(BF16))
        totals[i] = part if totals[i] is None else totals[i] + part
    return jnp.concatenate(totals, axis=1)


def finish(total, heads):
    width = heads * VDIM
    down = [total[width + head : width + head + 1, :] for head in range(heads)]
    return (total[:width, :] / spread(down, (width, total.shape[1]), heads)).astype(BF16)


def sources_of(shifts):
    here, count = lax.axis_index("tm"), lax.axis_size("tm")
    return [lax.rem(here + shift + count, count) for shift in shifts]


def pairs_of(refs):
    return list(zip(refs[::2], refs[1::2]))


def scaled_queries(mine_rows, their_rows, wq_ref, channels):
    mine, theirs = halves(channels)
    query = dot(mine_rows, wq_ref[mine, :]) + dot(their_rows, wq_ref[theirs, :])
    return jnp.transpose(query * (math.log2(math.e) / math.sqrt(QDIM)))


def query_kernel(mine_ref, theirs_ref, wq_ref, qt_ref):
    quarter, channels = mine_ref.shape
    queries = qt_ref.shape[1]
    blank = jnp.zeros((queries - quarter, channels), BF16)
    qt_ref[...] = scaled_queries(
        jnp.concatenate([mine_ref[...], blank], axis=0),
        jnp.concatenate([theirs_ref[...], blank], axis=0),
        wq_ref,
        channels,
    )


def own_kernel(heads, quarter, info_ref, qt_ref, first_ref, second_ref, bypass_hbm, *rest):
    sum_ref, bypass_ref, sem = rest[-3:]
    copy = pltpu.make_async_copy(bypass_hbm, bypass_ref, sem.at[0])
    copy.start()
    total = absorb(
        None, qt_ref[...], [(first_ref, second_ref)], sources_of([0]), info_ref[0:1, 0:1], quarter, heads
    )
    lane = lax.broadcasted_iota(jnp.int32, total.shape, 1)
    sum_ref[...] = jnp.where(lane < quarter, total, 0.0)
    copy.wait()


def open_kernel(heads, halo, shifts, info_ref, mine_ref, theirs_ref, wq_ref, qt_in_ref, sum_in_ref, *rest):
    packs = pairs_of(rest[: 2 * len(shifts)])
    rows_ref, qt_ref, sum_ref = rest[-3:]
    quarter, channels = mine_ref.shape
    first, second, _ = pack_plan(quarter, heads * VDIM)
    queries = rows_ref.shape[0]
    late = quarter - quarter % 128
    rows_ref[:quarter, :channels] = mine_ref[...]
    rows_ref[:quarter, channels:] = theirs_ref[...]
    rows_ref[quarter : quarter + halo, :] = get_edge(packs[1][1], second, halo, 2 * channels)
    rows_ref[quarter + halo : quarter + 2 * halo, :] = get_edge(packs[2][0], first, halo, 2 * channels)
    rows_ref[quarter + 2 * halo :, :] = jnp.zeros((queries - 2 * halo - quarter, 2 * channels), BF16)
    q_late = scaled_queries(rows_ref[late:, :channels], rows_ref[late:, channels:], wq_ref, channels)
    q_t = jnp.concatenate([qt_in_ref[:, :late], q_late], axis=1)
    qt_ref[...] = q_t
    live_rows = info_ref[0:1, 0:1]
    sources = sources_of(shifts)
    total = absorb(sum_in_ref[...], q_t, packs[1:], sources[1:], live_rows, quarter, heads)
    edge = absorb(None, q_late, packs[:1], sources[:1], live_rows, quarter, heads)
    lane = lax.broadcasted_iota(jnp.int32, edge.shape, 1) + late
    edge = jnp.where(lane < quarter, 0.0, edge)
    sum_ref[:, :late] = total[:, :late]
    sum_ref[:, late:] = total[:, late:] + edge


def more_kernel(heads, quarter, shifts, info_ref, qt_ref, sum_in_ref, *rest):
    packs = pairs_of(rest[: 2 * len(shifts)])
    sum_ref = rest[-1]
    sum_ref[...] = absorb(
        sum_in_ref[...], qt_ref[...], packs, sources_of(shifts), info_ref[0:1, 0:1], quarter, heads
    )


def close_kernel(heads, quarter, shifts, everything, info_ref, qt_ref, sum_in_ref, *rest):
    packs = pairs_of(rest[: 2 * len(shifts) + 2 * len(everything)])
    out_ref, held, total_ref = rest[-3:]
    live_rows = info_ref[0:1, 0:1]
    width = heads * VDIM
    total = absorb(
        sum_in_ref[...], qt_ref[...], packs[: len(shifts)], sources_of(shifts), live_rows, quarter, heads
    )
    out_ref[...] = finish(total, heads)
    down = total[width : width + heads, :]
    safe = jnp.where((down > 2.0**-60) & (down < 2.0**100), 0.0, 1.0)

    @pl.when(jnp.max(safe) > 0.0)
    def _():
        count = lax.axis_size("tm")
        first, second, _ = pack_plan(quarter, width)
        for i, (pack, shift) in enumerate(zip(packs, list(shifts) + list(everything))):
            held[i, :first, :] = pack[0][:first, :]
            held[i, first:, :] = pack[1][:second, :]
        firsts = sources_of(list(shifts) + list(everything))
        q_t = qt_ref[...]
        row = lax.broadcasted_iota(jnp.int32, (quarter, q_t.shape[1]), 0)
        total_ref[...] = jnp.zeros_like(total_ref)

        def first_row(i):
            first = firsts[0]
            for j in range(1, count):
                first = jnp.where(i == j, firsts[j], first)
            return first * quarter

        def one_head(head, carry):
            query = head_query(q_t, head)

            def scores(i):
                return jnp.where(row < live_rows - first_row(i), dot(held[i, :quarter, :], query), NEG)

            def highest(i, top):
                return jnp.maximum(top, jnp.max(scores(i), axis=0, keepdims=True))

            top = lax.fori_loop(0, count, highest, jnp.full((1, q_t.shape[1]), NEG, F32))

            def add(i, carry):
                expo = jnp.exp2(scores(i) - top).astype(BF16)
                values = all_values(held.at[i], quarter, first + second, quarter, width)
                values = head_values(values, head, live_rows - first_row(i))
                total_ref[...] += dot(values, expo)
                return carry

            return lax.fori_loop(0, count, add, carry)

        lax.fori_loop(0, heads, one_head, 0)
        out_ref[...] = finish(total_ref[...], heads)


def mix_kernel(rows_ref, attended_ref, w_out_ref, part_ref):
    channels = rows_ref.shape[1] // 2
    for side, lanes in zip(halves(channels), (slice(0, channels), slice(channels, 2 * channels))):
        delta = dot(attended_ref[...], w_out_ref[:, side], TN)
        part_ref[:, lanes] = rows_ref[:, lanes].astype(F32) + delta


def conv_kernel(
    halo, info_ref, part_ref, their_att_ref, their_out_ref, conv_in_ref, taps_ref,
    after_ref, hidden_ref, gated,
):
    quarter, channels = hidden_ref.shape
    taps = taps_ref.shape[0]
    count = quarter + 2 * halo
    mine, theirs = halves(channels)
    sides = []
    for side, lanes in ((mine, slice(0, channels)), (theirs, slice(channels, 2 * channels))):
        delta = dot(their_att_ref[...], their_out_ref[:, side], TN)
        sides.append((part_ref[:count, lanes] + delta[:count]).astype(BF16))
    after_ref[...] = sides[0][:quarter]
    gates = dot(sides[0], conv_in_ref[mine, :]) + dot(sides[1], conv_in_ref[theirs, :])
    value, gate = gates[:, :channels], gates[:, channels:]
    row = lax.broadcasted_iota(jnp.int32, (count, channels), 0)
    row = jnp.where((row >= quarter) & (row < quarter + halo), row - (quarter + halo), row)
    row = jnp.where(row >= quarter + halo, row - halo, row) + lax.axis_index("tm") * quarter
    live = (row >= 0) & (row < info_ref[0:1, 0:1])
    mixed = jnp.where(live, value * jax.nn.sigmoid(gate), 0.0).astype(BF16).astype(F32)
    for tile in range(channels // 128):
        lanes = slice(tile * 128, tile * 128 + 128)
        gated[tile, :halo] = mixed[quarter : quarter + halo, lanes]
        gated[tile, halo : halo + quarter] = mixed[:quarter, lanes]
        gated[tile, halo + quarter :] = mixed[quarter + halo :, lanes]
    block = 64
    start = halo - taps // 2
    for tile in range(channels // 128):
        lanes = slice(tile * 128, tile * 128 + 128)
        for base in range(0, quarter, block):
            total = None
            for k in range(taps):
                part = gated[tile, base + k + start : base + k + start + block, :] * taps_ref[k : k + 1, lanes]
                total = part if total is None else total + part
            hidden_ref[base : base + block, lanes] = (total * jax.nn.sigmoid(total)).astype(BF16)


def half_kernel(info_ref, after_ref, hidden_ref, out_w_ref, frames_ref, bypass_ref, base_ref, kept_ref):
    quarter, channels = hidden_ref.shape
    mine, _ = halves(channels)
    base_ref[...] = after_ref[...].astype(F32) + dot(hidden_ref[...], out_w_ref[:, mine])
    row = lax.broadcasted_iota(jnp.int32, (4 * quarter, 128), 0) + lax.axis_index("tm") * 4 * quarter
    live = row < info_ref[1:2, 0:1]
    for tile in range(channels // 128):
        lanes = slice(tile * 128, tile * 128 + 128)
        backdrop = frames_ref[:, lanes].astype(F32)
        kept_ref[tile] = jnp.where(live, backdrop - bypass_ref[:, lanes] * backdrop, 0.0)


def last_kernel(
    parts, info_ref, base_ref, hidden_ref, out_w_ref, kept_ref, bypass_ref, out_ref, tall, flat, sems
):
    quarter, channels = base_ref.shape
    rows = quarter // parts
    step = 4 * rows
    mine, _ = halves(channels)
    weights = out_w_ref[:, mine]
    length = info_ref[1:2, 0:1]
    row = lax.broadcasted_iota(jnp.int32, (step, 128), 0) + lax.axis_index("tm") * 4 * quarter
    copies = []
    for i in range(parts):
        part = slice(i * rows, (i + 1) * rows)
        span = slice(i * step, (i + 1) * step)
        stacked = bypass_ref[...] * (base_ref[part, :] + dot(hidden_ref[part, :], weights))
        live = row < length - i * step
        for tile in range(channels // 128):
            lanes = slice(tile * 128, tile * 128 + 128)
            for j in range(4):
                tall[tile, pl.ds(i * step + j, rows, stride=4), :] = stacked[:, lanes]
            added = jnp.where(live, tall[tile, span], 0.0)
            flat[span, lanes] = (kept_ref[tile, span] + added).astype(BF16)
        window = pl.ds(i * step, step)
        copies.append(pltpu.make_async_copy(flat.at[window], out_ref.at[window], sems.at[i]))
        copies[-1].start()
    for copy in copies:
        copy.wait()


def shards(
    frames,
    lengths,
    down_weights,
    w_query,
    w_key,
    w_value,
    w_out,
    conv_in,
    conv_taps,
    conv_out,
    bypass,
):
    records, frame_count, channels = frames.shape
    quarter = frame_count // 4
    heads = w_query.shape[1] // QDIM
    keys_wide = w_query.shape[1]
    count = lax.axis_size("tm")
    halo = -(-(conv_taps.shape[0] // 2) // 16) * 16
    queries = -(-(quarter + 2 * halo) // 128) * 128
    parts = quarter // 64
    frames = frames.reshape(frame_count, channels)
    swap = [(0, 1), (1, 0)]

    def ring(array, by):
        return lax.ppermute(array, "tm", [(i, (i + by) % count) for i in range(count)])

    def vmem(shape, dtype):
        return pltpu.VMEM(shape, dtype)

    reduced, info, kept_frames, kept_key, kept_value, kept_query = call(
        functools.partial(down_kernel, parts),
        [
            vmem((quarter, channels), BF16),
            vmem((8, 128), jnp.int32),
            vmem((frame_count, channels), BF16),
            vmem(w_key.shape, BF16),
            vmem(w_value.shape[::-1], BF16),
            vmem(w_query.shape, BF16),
        ],
        [lengths, frames, down_weights, w_key, w_value.T, w_query],
        [SM, HB, HB, HB, HB, HB],
        [
            pltpu.VMEM((channels // 128, frame_count, 128), F32),
            pltpu.VMEM(down_weights.shape, F32),
            pltpu.SemaphoreType.DMA((parts + 4,)),
        ],
        flops=8 * frame_count * channels,
        moved=3 * frame_count * channels,
    )
    theirs = lax.ppermute(reduced, "head", swap)
    width = heads * VDIM
    edge_rows = halo * 2 * channels // 128
    first_rows, second_rows, _ = pack_plan(quarter, width)
    first, second, first_left, second_right = call(
        functools.partial(kv_kernel, halo),
        [
            vmem((first_rows, keys_wide), BF16),
            vmem((second_rows, keys_wide), BF16),
            vmem((first_rows + edge_rows, keys_wide), BF16),
            vmem((second_rows + edge_rows, keys_wide), BF16),
        ],
        [reduced, theirs, kept_key, kept_value],
        [VM] * 4,
        flops=4 * quarter * channels * (keys_wide + width),
        moved=8 * quarter * channels,
    )
    reach = count // 2
    right_first, left_second = [ring(first, 1)], [ring(second, -1)]
    right_second, left_first = [ring(second_right, 1)], [ring(first_left, -1)]
    for step in range(2, reach + 1):
        right_first.append(ring(right_first[-1], 1))
        left_second.append(ring(left_second[-1], -1))
        if step < reach:
            right_second.append(ring(right_second[-1], 1))
            left_first.append(ring(left_first[-1], -1))
    their_w_out = lax.ppermute(w_out, "head", swap)
    their_conv_out = lax.ppermute(conv_out, "head", swap)
    gate_weights = conv_in.reshape(2 * channels, 2 * channels)
    early = [their_w_out, their_conv_out, gate_weights, conv_taps, w_out, conv_out]

    stages = [[(0, first, second), (-1, right_first[0], right_second[0]), (1, left_first[0], left_second[0])]]
    for step in range(2, reach):
        at = step - 1
        stages.append([(-step, right_first[at], right_second[at]), (step, left_first[at], left_second[at])])
    stages.append([(reach, right_first[-1], left_second[-1])])
    score_flops = 2 * quarter * queries * heads * (128 + 64)

    def arrays(stage):
        return [array for pack in stage for array in pack[1:]]

    def shifts(stage):
        return [pack[0] for pack in stage]

    (q_t,) = call(
        query_kernel,
        [vmem((keys_wide, queries), F32)],
        [reduced, theirs, kept_query],
        [VM] * 3,
        flops=4 * quarter * channels * keys_wide,
        moved=4 * quarter * channels,
    )
    total, bypass_row = call(
        functools.partial(own_kernel, heads, quarter),
        [vmem((width + 16, queries), F32), vmem((1, channels), F32)],
        [info, q_t, first, second, bypass.reshape(1, channels)] + early,
        [VM] * 4 + [HB] + [VM] * len(early),
        [pltpu.SemaphoreType.DMA((1,))],
        flops=score_flops,
        moved=quarter * queries * 4,
        exps=quarter * queries * heads,
    )
    rows, q_t, total = call(
        functools.partial(open_kernel, heads, halo, shifts(stages[0])),
        [
            vmem((queries, 2 * channels), BF16),
            vmem((keys_wide, queries), F32),
            vmem((width + 16, queries), F32),
        ],
        [info, reduced, theirs, kept_query, q_t, total] + arrays(stages[0]),
        [VM] * (6 + 2 * len(stages[0])),
        flops=score_flops * len(stages[0]),
        moved=quarter * queries * 4,
        exps=quarter * queries * heads * len(stages[0]),
    )
    for stage in stages[1:-1]:
        (total,) = call(
            functools.partial(more_kernel, heads, quarter, shifts(stage)),
            [vmem((width + 16, queries), F32)],
            [info, q_t, total] + arrays(stage),
            [VM] * (3 + 2 * len(stage)),
            flops=score_flops * len(stage),
            moved=quarter * queries * 4,
            exps=quarter * queries * heads * len(stage),
        )
    stage = stages[-1]
    others = [pack for group in stages[:-1] for pack in group]
    (attended,) = call(
        functools.partial(close_kernel, heads, quarter, shifts(stage), shifts(others)),
        [vmem((width, queries), BF16)],
        [info, q_t, total] + arrays(stage + others),
        [VM] * (3 + 2 * count),
        [
            pltpu.VMEM((count, first_rows + second_rows, keys_wide), BF16),
            pltpu.VMEM((width + 16, queries), F32),
        ],
        flops=score_flops * len(stage),
        moved=quarter * queries * 4,
        exps=quarter * queries * heads * len(stage),
    )
    their_attended = lax.ppermute(attended, "head", swap)
    (part,) = call(
        mix_kernel,
        [vmem((queries, 2 * channels), F32)],
        [rows, attended, w_out],
        [VM] * 3,
        flops=4 * queries * channels * width,
        moved=queries * channels * 8,
    )
    after, hidden = call(
        functools.partial(conv_kernel, halo),
        [vmem((quarter, channels), BF16), vmem((quarter, channels), BF16)],
        [info, part, their_attended, their_w_out, gate_weights, conv_taps],
        [VM] * 6,
        [pltpu.VMEM((channels // 128, quarter + 2 * halo, 128), F32)],
        flops=2 * queries * 2 * channels * (96 + 2 * channels),
        moved=quarter * channels * 8,
    )
    their_hidden = lax.ppermute(hidden, "head", swap)
    base, kept = call(
        half_kernel,
        [vmem((quarter, channels), F32), vmem((channels // 128, frame_count, 128), F32)],
        [info, after, hidden, conv_out, kept_frames, bypass_row],
        [VM] * 6,
        flops=2 * quarter * channels * channels,
        moved=quarter * channels * 4,
    )
    (out,) = call(
        functools.partial(last_kernel, parts),
        [jax.ShapeDtypeStruct((frame_count, channels), BF16)],
        [info, base, their_hidden, their_conv_out, kept, bypass_row],
        [VM] * 6,
        [
            pltpu.VMEM((channels // 128, frame_count, 128), F32),
            pltpu.VMEM((frame_count, channels), BF16),
            pltpu.SemaphoreType.DMA((parts,)),
        ],
        out_specs=[HB],
        flops=2 * quarter * channels * channels,
        moved=frame_count * channels * 4,
    )
    return out.reshape(records, frame_count, channels)


def solution(mesh):
    in_specs = (
        P(("groups", "dp"), "tm", "head"),
        P(("groups", "dp")),
        P(None, "head"),
        P(None, "head"),
        P(None, "head"),
        P(None, "head"),
        P("head", None),
        P(None, None, "head"),
        P(None, "head"),
        P("head", None),
        P("head"),
    )
    out_specs = P(("groups", "dp"), "tm", "head")
    return jax.shard_map(shards, mesh=mesh, in_specs=in_specs, out_specs=out_specs, check_vma=False)
```
